128 devices in a mesh: frame: 32 (over x, y, z_lo), row: 4 (over z_hi, core).
Axes of the slice: x: 4, y: 4, z: 4 (z_hi: 2, z_lo: 2; z = z_hi * 2 + z_lo), core: 2. Of those that a mesh axis runs over, the one named last changes fastest.
Arguments:
- query_pre: bfloat16 [2240, 32, 16, 128], P(None, 'frame', 'row'), may hold values from -6 to 6
- key_pre: bfloat16 [2240, 32, 16, 128], P(None, 'frame', 'row'), may hold values from -80 to 80
- values: bfloat16 [2240, 32, 16, 128], P(None, 'frame', 'row'), may hold values from -1 to 2
- cotangent: bfloat16 [2240, 32, 16, 128], P(None, 'frame', 'row'), may hold values from -3072 to 3072
- kernel: bfloat16 [3, 3, 2240], replicated, may hold values from -0.29882812 to 0.59765625
Outputs:
- grad_query: bfloat16 [2240, 32, 16, 128], P(None, 'frame', 'row')
- grad_key: bfloat16 [2240, 32, 16, 128], P(None, 'frame', 'row')
- grad_values: bfloat16 [2240, 32, 16, 128], P(None, 'frame', 'row')
The draws below stay inside these ranges and needn't reach their ends.
All inputs are finite; a program needn't handle non-finite values.
Results may differ from the reference program's by a relative error of at most 0.008.
Values may be sent and summed in bfloat16 or wider, within the bound.
A program may use at most 128 MiB of HBM per device.

```python
import jax
import jax.numpy as jnp
from jax import lax

HEADS = 70
HD = 32
D = 2240
COLS = 128
NF = 32
NR = 16
NTOK = 65536


def draw_key_pre(key, part):
    first, second, third = jax.random.split(jax.random.fold_in(key, 17), 3)
    frame_pos = jnp.arange(NF, dtype=jnp.float32) / max(NF - 1, 1)
    base = jnp.clip(jax.random.normal(first, (D, NF, NR, COLS), jnp.float32), -4.0, 4.0)
    ramp = jnp.exp(jnp.log(3.0) * frame_pos)
    channel_scale = jnp.exp(jax.random.uniform(second, (D,), jnp.float32, -1.15, 1.15))
    frame_scale = ramp * jnp.exp(jax.random.uniform(third, (NF,), jnp.float32, -0.7, 0.7))
    drawn = base * channel_scale[:, None, None, None] * frame_scale[None, :, None, None]
    return drawn.astype(jnp.bfloat16)


def levels(key, extent, shards, least, largest):
    gain, own = 1.0, jax.random.fold_in(key, 6)
    for axis_at, parts in shards:
        draws = jnp.exp(jax.random.uniform(jax.random.fold_in(own, axis_at), (parts,), jnp.float32, least / len(shards), largest / len(shards)))
        gain = gain * jnp.repeat(draws, extent[axis_at] // parts).reshape([-1 if axis == axis_at else 1 for axis in range(len(extent))])
    return gain


def gaussian(own_key, shape, spread, limit, cuts=(), kind=jnp.bfloat16):
    values = spread * jax.random.normal(own_key, shape, jnp.float32)
    if cuts:
        values = values * levels(own_key, shape, cuts, -0.22, 0.18)
    return jnp.clip(values, -limit, limit).astype(kind)


def setup_inputs(seed: int = 0) -> dict:
    arg_keys = jax.random.split(jax.random.key(seed), 6)
    query_pre = gaussian(arg_keys[0], (D, NF, NR, COLS), 1.0, 6.0, ((1, 32), (2, 4)))
    key_pre = draw_key_pre(jax.random.fold_in(arg_keys[5], 71), 0)
    values = jnp.clip(-1.0 + 3.0 * jax.random.uniform(arg_keys[2], (D, NF, NR, COLS), jnp.float32) ** levels(arg_keys[2], (D, NF, NR, COLS), ((1, 32), (2, 4)), -0.2, 0.2), -1.0, 2.0).astype(jnp.bfloat16)
    cotangent = gaussian(arg_keys[3], (D, NF, NR, COLS), (2 * NTOK ** 0.5), 3072.0, ((1, 32), (2, 4)))
    kernel = jnp.clip(jax.random.uniform(arg_keys[4], (3, 3, D), jnp.float32, -0.29882812, 0.59765625), -0.29882812, 0.59765625).astype(jnp.bfloat16)
    return {"query_pre": query_pre, "key_pre": key_pre, "values": values, "cotangent": cotangent, "kernel": kernel}


denominator_eps = 1e-3


def conv_taps(padded, weights, flipped, row_count, col_count):
    summed = None
    for tap_row in range(3):
        for tap_col in range(3):
            start_row = 2 - tap_row if flipped else tap_row
            start_col = 2 - tap_col if flipped else tap_col
            window = padded[:, :, start_row:start_row + row_count, start_col:start_col + col_count]
            tap_term = weights[tap_row, tap_col][:, None, None, None] * window
            summed = tap_term if summed is None else summed + tap_term
    return summed


def one_head(pieces):
    query_h, key_h, value_h, cot_h, weight_h = pieces
    highest = lax.Precision.HIGHEST
    weight_f = weight_h.astype(jnp.float32)
    value_pad = jnp.pad(value_h.astype(jnp.float32), ((0, 0), (0, 0), (1, 1), (1, 1)))
    mixed = conv_taps(value_pad, weight_f, False, NR, COLS).reshape(HD, -1)
    key_act = jax.nn.relu(key_h.astype(jnp.float32)).reshape(HD, -1)
    query_act = jax.nn.relu(query_h.astype(jnp.float32)).reshape(HD, -1)
    state = jnp.einsum("jt,et->je", key_act, mixed, precision=highest)
    key_sum = jnp.sum(key_act, axis=1)
    denom = jnp.einsum("j,jt->t", key_sum, query_act, precision=highest) + denominator_eps * NTOK
    numer = jnp.einsum("je,jt->et", state, query_act, precision=highest)
    output = numer / denom[None, :]
    grad_out = cot_h.astype(jnp.float32).reshape(HD, -1)
    grad_num = grad_out / denom[None, :]
    grad_den = -jnp.sum(grad_out * output, axis=0) / denom
    grad_state = jnp.einsum("jt,et->je", query_act, grad_num, precision=highest)
    grad_sum = jnp.einsum("jt,t->j", query_act, grad_den, precision=highest)
    grad_qact = jnp.einsum("je,et->jt", state, grad_num, precision=highest) + key_sum[:, None] * grad_den[None, :]
    grad_query = jnp.where(query_h.reshape(HD, -1) > 0, grad_qact, 0.0).astype(jnp.bfloat16)
    grad_mixed = jnp.einsum("je,jt->et", grad_state, key_act, precision=highest)
    grad_kact = jnp.einsum("je,et->jt", grad_state, mixed, precision=highest) + grad_sum[:, None]
    grad_key = jnp.where(key_h.reshape(HD, -1) > 0, grad_kact, 0.0).astype(jnp.bfloat16)
    grad_pad = jnp.pad(grad_mixed.reshape(HD, NF, NR, COLS), ((0, 0), (0, 0), (1, 1), (1, 1)))
    grad_values = conv_taps(grad_pad, weight_f, True, NR, COLS).astype(jnp.bfloat16)
    return (grad_query.reshape(HD, NF, NR, COLS), grad_key.reshape(HD, NF, NR, COLS), grad_values)


def reference(query_pre, key_pre, values, cotangent, kernel):
    shape_h = (HEADS, HD, NF, NR, COLS)
    head_kernel = kernel.reshape(3, 3, HEADS, HD).transpose(2, 0, 1, 3)
    grad_query, grad_key, grad_values = lax.map(one_head, (query_pre.reshape(shape_h), key_pre.reshape(shape_h), values.reshape(shape_h), cotangent.reshape(shape_h), head_kernel))
    full_shape = (D, NF, NR, COLS)
    return (grad_query.reshape(full_shape), grad_key.reshape(full_shape), grad_values.reshape(full_shape))
```

```python
import functools

import jax
import jax.numpy as jnp
from jax import lax
from jax.experimental import pallas as pl
from jax.experimental.pallas import tpu as pltpu
from jax.sharding import PartitionSpec as P

HD = 32
HPG = 7
GC = HPG * HD
GK = 256
COLS = 128
ROWS = 4
UNITS = 16
EPS = 0.001
MESH = pl.DeviceIdType.MESH
F32 = jnp.float32
BF16 = jnp.bfloat16


def lanes(shape):
    return lax.broadcasted_iota(jnp.int32, shape, len(shape) - 1)


def conv16(rows, weights, flipped):
    lane = lanes((16, COLS))
    taps = [jnp.broadcast_to(weights[:, i : i + 1], (16, COLS)) for i in range(9)]
    outs = []
    for r in range(ROWS):
        sums = []
        for b in range(3):
            total = None
            for a in range(3):
                at = (2 - a) * 3 + (2 - b) if flipped else a * 3 + b
                term = taps[at] * rows[r + a]
                total = term if total is None else total + term
            sums.append(total)
        before = jnp.where(lane >= 1, pltpu.roll(sums[0], 1, 1), 0.0)
        after = jnp.where(lane < COLS - 1, pltpu.roll(sums[2], COLS - 1, 1), 0.0)
        outs.append(sums[1] + before + after)
    return outs


def pack(full):
    lane = lanes((HD, 128))
    block = lax.shift_right_logical(lane, 5)
    first = jnp.zeros((HD, 128), F32)
    second = jnp.zeros((HD, 128), F32)
    for h in range(HPG):
        rows = slice(HD * h, HD * h + HD)
        if h < 4:
            first = jnp.where(block == h, full[rows, :128], first)
        else:
            second = jnp.where(block == h - 4, full[rows, 128:], second)
        second = jnp.where(lane == 96 + h, full[rows, 128:], second)
    return first, second


def put_units(ref, at, packed):
    for t, part in enumerate(packed):
        for k in range(8):
            ref[at + t * 8 + k] = part[4 * k : 4 * k + 4]


def take_units(ref, at):
    halves = [
        jnp.concatenate([ref[at + t * 8 + k] for k in range(8)], axis=0) for t in range(2)
    ]
    return jnp.concatenate(halves, axis=1)


def spread(packed, keep_sums):
    stacked = jnp.concatenate([packed] * HPG, axis=0)
    head = lax.shift_right_logical(lax.broadcasted_iota(jnp.int32, (GC, GK), 0), 5)
    lane = lanes((GC, GK))
    keep = head == lax.shift_right_logical(lane, 5)
    if keep_sums:
        keep = keep | (lane == GC + head)
    return jnp.where(keep, stacked, 0.0)


def first_kernel(
    frames, rows, all_tokens,
    q_hbm, k_hbm, v_hbm, c_hbm, w_ref,
    state_out, mixed_out, key_out, query_out, weights_out,
    qn, kn, vn, cn, wide, vpl, vedge, vhalo, kp, qp, cp, mf, mx, wt,
    part1, part2, got1, got2, all1, all2, means, qout,
    in_sem, out_sem, vsend, vrecv, ksend, krecv, s_sem, r_sem, g_sem, a_sem,
):
    groups = vpl.shape[0] // GC
    n_dev = frames * rows
    frame, row = lax.axis_index("frame"), lax.axis_index("row")
    me = frame * rows + row
    has_up, has_down = row > 0, row < rows - 1
    n_units = groups * UNITS
    extra = n_units - n_dev

    def device(d):
        return (d // rows, lax.rem(d, rows))

    sources = ((v_hbm, vn), (k_hbm, kn), (q_hbm, qn), (c_hbm, cn))

    def load(i, g):
        src, dst = sources[i]
        at = pl.ds(pl.multiple_of(g * GC * ROWS, GC * ROWS), GC * ROWS)
        return pltpu.make_async_copy(src.at[at], dst.at[at], in_sem.at[i, g])

    for i in range(4):

        @pl.loop(0, groups)
        def _(g):
            load(i, g).start()

    barrier = pltpu.get_barrier_semaphore()

    @pl.loop(1, n_dev)
    def _(i):
        d = lax.rem(me + i, n_dev)
        pl.semaphore_signal(barrier, inc=1, device_id=device(d), device_id_type=MESH)

    taps = jnp.concatenate([w_ref[a].astype(F32) for a in range(3)], axis=0)
    taps = jnp.concatenate([taps, jnp.zeros((7, taps.shape[1]), F32)], axis=0)
    channels = taps.shape[1]
    for at in range(0, channels, 128):
        size = min(128, channels - at)
        wt[at : at + size, :] = jnp.concatenate(
            [taps[:, at : at + size].T, jnp.zeros((size, 112), F32)], axis=1
        )

    def planes(nat, g):
        at = pl.multiple_of(g * GC * ROWS, GC * ROWS)
        wide[...] = nat[pl.ds(at, GC * ROWS), :].astype(F32)
        return [wide[pl.ds(r, GC, stride=ROWS), :] for r in range(ROWS)]

    def at_group(g, size=GC):
        return pl.ds(pl.multiple_of(g * size, size), size)

    @pl.loop(0, groups)
    def _(g):
        load(0, g).wait()
        rows4 = planes(vn, g)
        for r in range(ROWS):
            vpl[at_group(g), COLS * r : COLS * r + COLS] = rows4[r]
        vedge[0, at_group(g), :] = rows4[0].astype(BF16)
        vedge[1, at_group(g), :] = rows4[3].astype(BF16)

    zero_plane = jnp.zeros((GC, COLS), BF16)

    @pl.when(jnp.logical_not(has_up))
    def _():
        @pl.loop(0, groups)
        def _(g):
            vhalo[0, at_group(g), :] = zero_plane
            kp[at_group(g), 0:COLS] = zero_plane

    @pl.when(jnp.logical_not(has_down))
    def _():
        @pl.loop(0, groups)
        def _(g):
            vhalo[1, at_group(g), :] = zero_plane
            kp[at_group(g), 5 * COLS : 6 * COLS] = zero_plane

    pl.semaphore_wait(barrier, n_dev - 1)

    def value_halo(way, g):
        return pltpu.make_async_remote_copy(
            src_ref=vedge.at[way, at_group(g), :],
            dst_ref=vhalo.at[1 - way, at_group(g), :],
            send_sem=vsend.at[way],
            recv_sem=vrecv.at[1 - way, g],
            device_id=(frame, row - 1 if way == 0 else row + 1),
            device_id_type=MESH,
        )

    def key_halo(way, g):
        src = COLS if way == 0 else 4 * COLS
        dst = 5 * COLS if way == 0 else 0
        return pltpu.make_async_remote_copy(
            src_ref=kp.at[at_group(g), src : src + COLS],
            dst_ref=kp.at[at_group(g), dst : dst + COLS],
            send_sem=ksend.at[way],
            recv_sem=krecv.at[1 - way, g],
            device_id=(frame, row - 1 if way == 0 else row + 1),
            device_id_type=MESH,
        )

    def send_halos(halo):
        for way, there in ((0, has_up), (1, has_down)):

            @pl.when(there)
            def _():
                @pl.loop(0, groups)
                def _(g):
                    halo(way, g).start()

    def wait_halo(halo, g):
        for way, there in ((1, has_up), (0, has_down)):

            @pl.when(there)
            def _():
                halo(way, g).wait_recv()

    def wait_sent(sem):
        for way, there in ((0, has_up), (1, has_down)):

            @pl.when(there)
            def _():
                pltpu.make_async_copy(vedge.at[way], vedge.at[way], sem.at[way]).wait()

    send_halos(value_halo)

    @pl.loop(0, groups)
    def _(g):
        load(1, g).wait()
        rows4 = planes(kn, g)
        for r in range(ROWS):
            kp[at_group(g), COLS * (r + 1) : COLS * (r + 2)] = jnp.maximum(
                rows4[r], 0.0
            ).astype(BF16)
        mx[pl.ds(pl.multiple_of(g * GK + GC, 32), GK - GC), :] = jnp.ones(
            (GK - GC, ROWS * COLS), BF16
        )

    @pl.loop(0, groups)
    def _(g):
        load(2, g).wait()
        rows4 = planes(qn, g)
        for r in range(ROWS):
            qp[at_group(g), COLS * r : COLS * (r + 1)] = jnp.maximum(rows4[r], 0.0).astype(BF16)

    @pl.loop(0, groups)
    def _(g):
        load(3, g).wait()
        rows4 = planes(cn, g)
        top = pl.ds(pl.multiple_of(g * GK, GK), GC)
        for r in range(ROWS):
            cp[top, COLS * r : COLS * (r + 1)] = rows4[r].astype(BF16)
        cp[pl.ds(pl.multiple_of(g * GK + GC, 32), GK - GC), :] = jnp.zeros(
            (GK - GC, ROWS * COLS), BF16
        )

    def owner(u):
        f = u - n_dev
        second = u >= n_dev
        return jnp.where(second, f * rows + lax.rem(f, rows), u), jnp.where(second, 1, 0)

    owns_two = (row == lax.rem(frame, rows)) & (frame < extra)
    second_unit = n_dev + frame

    def scatter(part, got, at, g):
        @pl.loop(0, UNITS)
        def _(i):
            u = g * UNITS + i
            d, slot = owner(u)

            @pl.when(d != me)
            def _():
                pltpu.make_async_remote_copy(
                    src_ref=part.at[u],
                    dst_ref=got.at[slot * n_dev + me],
                    send_sem=s_sem.at[at],
                    recv_sem=r_sem.at[at, slot],
                    device_id=device(d),
                    device_id_type=MESH,
                ).start()

            @pl.when(d == me)
            def _():
                got[slot * n_dev + me] = part[u]

    def wait_bytes(ref, count, sem):
        pltpu.make_async_copy(ref.at[pl.ds(0, count)], ref.at[pl.ds(0, count)], sem).wait()

    def gather(got, every, at):
        def one(slot, u):
            wait_bytes(got, n_dev - 1, r_sem.at[at, slot])
            every[u] = jnp.sum(got[slot * n_dev : (slot + 1) * n_dev], axis=0)

            @pl.loop(1, n_dev)
            def _(i):
                d = lax.rem(me + i, n_dev)
                pltpu.make_async_remote_copy(
                    src_ref=every.at[u],
                    dst_ref=every.at[u],
                    send_sem=g_sem.at[at],
                    recv_sem=a_sem.at[at, slot],
                    device_id=device(d),
                    device_id_type=MESH,
                ).start()

        one(0, me)

        @pl.when(owns_two)
        def _():
            one(1, second_unit)

    def wait_gathered(every, at):
        wait_bytes(every, n_dev - 1, a_sem.at[at, 0])

        @pl.when(owns_two)
        def _():
            wait_bytes(every, extra - 1, a_sem.at[at, 1])

        @pl.when(jnp.logical_not(owns_two))
        def _():
            wait_bytes(every, extra, a_sem.at[at, 1])

    def wait_sends(at):
        @pl.when(owns_two)
        def _():
            wait_bytes(part1, n_units - 2, s_sem.at[at])
            wait_bytes(got1, 2 * (n_dev - 1), g_sem.at[at])

        @pl.when(jnp.logical_not(owns_two))
        def _():
            wait_bytes(part1, n_units - 1, s_sem.at[at])
            wait_bytes(got1, n_dev - 1, g_sem.at[at])

    @pl.loop(0, groups)
    def _(g):
        wait_halo(value_halo, g)

        @pl.loop(0, GC // 16)
        def _(i):
            c = pl.ds(pl.multiple_of(g * GC + i * 16, 16), 16)
            six = [vhalo[0, c, :].astype(F32)]
            six += [vpl[c, COLS * r : COLS * (r + 1)] for r in range(ROWS)]
            six += [vhalo[1, c, :].astype(F32)]
            outs = conv16(six, wt[c, :], False)
            o = pl.ds(pl.multiple_of(g * GK + i * 16, 16), 16)
            for r in range(ROWS):
                mf[c, COLS * r : COLS * (r + 1)] = outs[r]
                mx[o, COLS * r : COLS * (r + 1)] = outs[r].astype(BF16)

        full = lax.dot_general(
            kp[at_group(g), COLS : 5 * COLS],
            mx[at_group(g, GK), :],
            (((1,), (1,)), ((), ())),
            preferred_element_type=F32,
        )
        put_units(part1, g * UNITS, pack(full))
        scatter(part1, got1, 0, g)

    send_halos(key_halo)
    weights_copy = pltpu.make_async_copy(wt, weights_out, out_sem.at[0])
    weights_copy.start()
    gather(got1, all1, 0)
    wait_gathered(all1, 0)

    @pl.loop(0, groups)
    def _(g):
        packed = take_units(all1, g * UNITS)
        lane = lanes((HD, GK))
        head = lax.shift_right_logical(lane, 5)
        sums = [packed[:, GC + h : GC + h + 1] for h in range(HPG)]
        sums_wide = jnp.zeros((HD, GK), F32)
        for h in range(HPG):
            sums_wide = jnp.where(head == h, sums[h], sums_wide)
        total = jnp.sum(packed, axis=0, keepdims=True)
        weight = jnp.sum(sums_wide, axis=0, keepdims=True)
        mean = total / (weight + EPS * all_tokens)
        mean = jnp.where(lanes((1, GK)) < GC, mean, 0.0)
        means[g] = jnp.broadcast_to(mean, (8, GK))
        centred = spread(packed - sums_wide * mean, False)
        mean_rows = jnp.where(
            lax.shift_right_logical(lanes((16, GK)), 5)
            == lax.broadcasted_iota(jnp.int32, (16, GK), 0),
            mean,
            0.0,
        )
        left = jnp.concatenate([centred, mean_rows], axis=0).astype(BF16)
        cot = cp[at_group(g, GK), :]
        prod = jnp.dot(left, cot, preferred_element_type=F32)
        stacked = jnp.concatenate([jnp.broadcast_to(s, (HD, 128)) for s in sums], axis=0)
        by_head = jnp.where(
            lanes((GC, 128))
            == lax.shift_right_logical(lax.broadcasted_iota(jnp.int32, (GC, 128), 0), 5),
            stacked,
            0.0,
        )
        sums_rows = by_head.T[:16]
        high = sums_rows.astype(BF16)
        low = (sums_rows - high.astype(F32)).astype(BF16)
        qa = qp[at_group(g), :]
        both = jnp.dot(
            jnp.concatenate([high, low], axis=0), qa, preferred_element_type=F32
        )
        denom = both[:16] + both[16:] + EPS * all_tokens
        inv = 1.0 / denom
        down_rows = []
        scaled = []
        for h in range(HPG):
            rows_h = slice(HD * h, HD * h + HD)
            qh = qa[rows_h].astype(F32)
            ph = prod[rows_h]
            dot_h = jnp.sum(qh * ph, axis=0, keepdims=True)
            inv_h = inv[h : h + 1]
            down = -(dot_h - EPS * all_tokens * prod[GC + h : GC + h + 1]) * inv_h
            down_rows.append(down)
            grad = ph * inv_h + stacked[rows_h, 0:1] * (down * inv_h)
            grad = jnp.where(qh > 0, grad, 0.0)
            scaled.append((qh * inv_h).astype(BF16))
            for r in range(ROWS):
                wide[pl.ds(h * HD * ROWS + r, HD, stride=ROWS), :] = grad[
                    :, COLS * r : COLS * (r + 1)
                ]
        nat = pl.ds(pl.multiple_of(g * GC * ROWS, GC * ROWS), GC * ROWS)
        qout[nat, :] = wide[...].astype(BF16)
        tail = jnp.concatenate(down_rows + [jnp.zeros((GK - GC - HPG, ROWS * COLS), F32)], axis=0)
        right = jnp.concatenate([cot[:GC], tail.astype(BF16)], axis=0)
        full = lax.dot_general(
            jnp.concatenate(scaled, axis=0),
            right,
            (((1,), (1,)), ((), ())),
            preferred_element_type=F32,
        )
        put_units(part2, g * UNITS, pack(full))
        scatter(part2, got2, 1, g)

    query_copy = pltpu.make_async_copy(qout, query_out, out_sem.at[1])
    query_copy.start()

    @pl.loop(0, groups)
    def _(g):
        column = means[g].T[:GC, 0:1]
        o = pl.ds(pl.multiple_of(g * GK, GK), GC)
        mx[o, :] = (mf[at_group(g), :] - column).astype(BF16)
        wait_halo(key_halo, g)

    mixed_copy = pltpu.make_async_copy(mx, mixed_out, out_sem.at[2])
    mixed_copy.start()
    key_copy = pltpu.make_async_copy(kp, key_out, out_sem.at[3])
    key_copy.start()

    gather(got2, all2, 1)
    wait_gathered(all2, 1)
    state_copy = pltpu.make_async_copy(all2, state_out, out_sem.at[4])
    state_copy.start()
    wait_sent(vsend)
    wait_sent(ksend)
    wait_sends(0)
    wait_sends(1)
    weights_copy.wait()
    query_copy.wait()
    mixed_copy.wait()
    key_copy.wait()
    state_copy.wait()


def second_kernel(state, mixed, keys, weights, query_in, gq, gk, gv, wide, mapped):
    gq[...] = query_in[...]
    packed = take_units(state, 0)
    left = spread(packed, True).astype(BF16)
    grad_key = jnp.dot(left, mixed[...], preferred_element_type=F32)
    for r in range(ROWS):
        part = grad_key[:, COLS * r : COLS * (r + 1)]
        wide[pl.ds(r, GC, stride=ROWS), :] = jnp.where(
            keys[:, COLS * (r + 1) : COLS * (r + 2)].astype(F32) > 0, part, 0.0
        )
    gk[...] = wide[...].astype(BF16)
    turned = jnp.concatenate([packed] * 4, axis=0).T[:GC]
    turned = jnp.concatenate([turned, turned], axis=1)
    head = lax.shift_right_logical(lax.broadcasted_iota(jnp.int32, (GC, GK), 0), 5)
    turned = jnp.where(head == lax.shift_right_logical(lanes((GC, GK)), 5), turned, 0.0)
    mapped[...] = jnp.dot(
        turned[:, :GC].astype(BF16), keys[...], preferred_element_type=F32
    )

    @pl.loop(0, GC // 16)
    def _(i):
        c = pl.ds(pl.multiple_of(i * 16, 16), 16)
        six = [mapped[c, COLS * r : COLS * (r + 1)] for r in range(ROWS + 2)]
        outs = conv16(six, weights[c, :], True)
        for r in range(ROWS):
            wide[pl.ds(i * 16 * ROWS + r, 16, stride=ROWS), :] = outs[r]

    gv[...] = wide[...].astype(BF16)


def shards(frames, rows, query_pre, key_pre, values, cotangent, kernel):
    channels = values.shape[0]
    groups = channels // GC
    flat = (channels * ROWS, COLS)
    tokens = ROWS * COLS
    all_tokens = tokens * frames * rows
    n_units = groups * UNITS
    n_dev = frames * rows
    hbm = pl.BlockSpec(memory_space=pl.ANY)
    unit = (4, 128)
    state, mixed, keys, query, weights = pl.pallas_call(
        functools.partial(first_kernel, frames, rows, all_tokens),
        out_shape=(
            jax.ShapeDtypeStruct((n_units, *unit), F32),
            jax.ShapeDtypeStruct((groups * GK, tokens), BF16),
            jax.ShapeDtypeStruct((channels, 6 * COLS), BF16),
            jax.ShapeDtypeStruct(flat, BF16),
            jax.ShapeDtypeStruct((channels, 128), F32),
        ),
        in_specs=[hbm] * 4 + [pl.BlockSpec(memory_space=pltpu.VMEM)],
        out_specs=(hbm,) * 5,
        scratch_shapes=[
            pltpu.VMEM(flat, BF16),
            pltpu.VMEM(flat, BF16),
            pltpu.VMEM(flat, BF16),
            pltpu.VMEM(flat, BF16),
            pltpu.VMEM((GC * ROWS, COLS), F32),
            pltpu.VMEM((channels, tokens), F32),
            pltpu.VMEM((2, channels, COLS), BF16),
            pltpu.VMEM((2, channels, COLS), BF16),
            pltpu.VMEM((channels, 6 * COLS), BF16),
            pltpu.VMEM((channels, tokens), BF16),
            pltpu.VMEM((groups * GK, tokens), BF16),
            pltpu.VMEM((channels, tokens), F32),
            pltpu.VMEM((groups * GK, tokens), BF16),
            pltpu.VMEM((channels, 128), F32),
            pltpu.VMEM((n_units, *unit), F32),
            pltpu.VMEM((n_units, *unit), F32),
            pltpu.VMEM((2 * n_dev, *unit), F32),
            pltpu.VMEM((2 * n_dev, *unit), F32),
            pltpu.VMEM((n_units, *unit), F32),
            pltpu.VMEM((n_units, *unit), F32),
            pltpu.VMEM((groups, 8, GK), F32),
            pltpu.VMEM(flat, BF16),
            pltpu.SemaphoreType.DMA((4, groups)),
            pltpu.SemaphoreType.DMA((5,)),
            pltpu.SemaphoreType.DMA((2,)),
            pltpu.SemaphoreType.DMA((2, groups)),
            pltpu.SemaphoreType.DMA((2,)),
            pltpu.SemaphoreType.DMA((2, groups)),
            pltpu.SemaphoreType.DMA((2,)),
            pltpu.SemaphoreType.DMA((2, 2)),
            pltpu.SemaphoreType.DMA((2,)),
            pltpu.SemaphoreType.DMA((2, 2)),
        ],
        compiler_params=pltpu.CompilerParams(
            collective_id=0, has_side_effects=True, vmem_limit_bytes=56 * 2**20
        ),
    )(
        query_pre.reshape(flat),
        key_pre.reshape(flat),
        values.reshape(flat),
        cotangent.reshape(flat),
        kernel,
    )
    nat = pl.BlockSpec((GC * ROWS, COLS), lambda g: (g, 0))
    gq, gk, gv = pl.pallas_call(
        second_kernel,
        grid=(groups,),
        out_shape=(jax.ShapeDtypeStruct(flat, BF16),) * 3,
        in_specs=[
            pl.BlockSpec((UNITS, *unit), lambda g: (g, 0, 0)),
            pl.BlockSpec((GK, tokens), lambda g: (g, 0)),
            pl.BlockSpec((GC, 6 * COLS), lambda g: (g, 0)),
            pl.BlockSpec((GC, 128), lambda g: (g, 0)),
            nat,
        ],
        out_specs=(nat,) * 3,
        scratch_shapes=[
            pltpu.VMEM((GC * ROWS, COLS), F32),
            pltpu.VMEM((GC, 6 * COLS), F32),
        ],
    )(state, mixed, keys, weights, query)
    return tuple(o.reshape(values.shape) for o in (gq, gk, gv))


def solution(mesh):
    frames, rows = mesh.shape["frame"], mesh.shape["row"]
    spec = P(None, "frame", "row", None)
    return jax.shard_map(
        functools.partial(shards, frames, rows),
        mesh=mesh,
        in_specs=(spec, spec, spec, spec, P()),
        out_specs=(spec, spec, spec),
        check_vma=False,
    )
```

```python
import functools

import jax
import jax.numpy as jnp
from jax import lax
from jax.experimental import pallas as pl
from jax.experimental.pallas import tpu as pltpu
from jax.sharding import PartitionSpec as P

HD = 32
HPG = 7
GC = HPG * HD
GK = 256
COLS = 128
ROWS = 4
UNITS = 16
EPS = 0.001
UNROLL = 14
MESH = pl.DeviceIdType.MESH
FLAT = pl.DeviceIdType.LOGICAL
F32 = jnp.float32
BF16 = jnp.bfloat16


def lanes(shape):
    return lax.broadcasted_iota(jnp.int32, shape, len(shape) - 1)


def conv16(rows, weights, flipped):
    lane = lanes((16, COLS))
    taps = [weights[:, COLS * i : COLS * i + COLS].astype(F32) for i in range(9)]
    for i in range(9):
        b = 2 - i % 3 if flipped else i % 3
        if b != 1:
            taps[i] = jnp.where(lane == (COLS - 1 if b == 0 else 0), 0.0, taps[i])
    outs = []
    for r in range(ROWS):
        sums = []
        for b in range(3):
            total = None
            for a in range(3):
                at = (2 - a) * 3 + (2 - b) if flipped else a * 3 + b
                term = taps[at] * rows[r + a]
                total = term if total is None else total + term
            sums.append(total)
        outs.append(sums[1] + pltpu.roll(sums[0], 1, 1) + pltpu.roll(sums[2], COLS - 1, 1))
    return outs


def pack(full):
    lane = lanes((HD, 128))
    block = lax.shift_right_logical(lane, 5)
    first = jnp.zeros((HD, 128), F32)
    second = jnp.zeros((HD, 128), F32)
    for h in range(HPG):
        rows = slice(HD * h, HD * h + HD)
        if h < 4:
            first = jnp.where(block == h, full[rows, :128], first)
        else:
            second = jnp.where(block == h - 4, full[rows, 128:], second)
        second = jnp.where(lane == 96 + h, full[rows, 128:], second)
    return first, second


def put_units(ref, at, packed):
    for t, part in enumerate(packed):
        for k in range(8):
            ref[at + t * 8 + k] = part[4 * k : 4 * k + 4]


def take_units(ref, at):
    halves = [
        jnp.concatenate([ref[at + t * 8 + k] for k in range(8)], axis=0) for t in range(2)
    ]
    return jnp.concatenate(halves, axis=1)


def spread(packed, keep_sums):
    stacked = jnp.concatenate([packed] * HPG, axis=0)
    head = lax.shift_right_logical(lax.broadcasted_iota(jnp.int32, (GC, GK), 0), 5)
    lane = lanes((GC, GK))
    keep = head == lax.shift_right_logical(lane, 5)
    if keep_sums:
        keep = keep | (lane == GC + head)
    return jnp.where(keep, stacked, 0.0)


def first_kernel(
    frames, rows, all_tokens,
    q_hbm, k_hbm, v_hbm, c_hbm, w_ref,
    state_out, mixed_out, key_out, query_out, weights_out,
    qn, kn, vn, cn, wide, vpl, vedge, vhalo, kp, qp, cp, mf, mx, wt, wb, hot, sums, invs, downs,
    part1, part2, got1, got2, all1, all2, means, qout,
    here, in_sem, out_sem, vsend, vrecv, ksend, krecv, s_sem, r_sem, g_sem, a_sem,
):
    groups = vpl.shape[0] // GC
    n_dev = frames * rows
    frame, row = lax.axis_index("frame"), lax.axis_index("row")
    me = frame * rows + row
    has_up, has_down = row > 0, row < rows - 1
    n_units = groups * UNITS
    extra = n_units - n_dev

    def others(act):
        def one(i):
            d = me + i
            act(jnp.where(d >= n_dev, d - n_dev, d))

        @pl.loop(0, (n_dev - 2) // 9)
        def _(step):
            for i in range(9):
                one(step * 9 + i + 1)

        one(n_dev - 1)

    sources = ((v_hbm, vn), (k_hbm, kn), (q_hbm, qn), (c_hbm, cn))

    def load(i, g):
        src, dst = sources[i]
        at = pl.ds(pl.multiple_of(g * GC * ROWS, GC * ROWS), GC * ROWS)
        return pltpu.make_async_copy(src.at[at], dst.at[at], in_sem.at[i, g])

    for i in range(4):

        @pl.loop(0, groups)
        def _(g):
            load(i, g).start()

    barrier = pltpu.get_barrier_semaphore()

    lines = ((1, rows), (rows, 2), (2 * rows, 4), (8 * rows, 4))

    def signal_line(sem, line):
        stride, length = line
        at = lax.rem(me // stride, length)
        for i in range(1, length):
            to = me + (lax.rem(at + i, length) - at) * stride
            pl.semaphore_signal(sem, inc=1, device_id=to, device_id_type=FLAT)

    for line in lines:
        signal_line(barrier, line)

    def planes(nat, g):
        at = pl.multiple_of(g * GC * ROWS, GC * ROWS)
        wide[...] = nat[pl.ds(at, GC * ROWS), :].astype(F32)
        return [wide[pl.ds(r, GC, stride=ROWS), :] for r in range(ROWS)]

    def at_group(g, size=GC):
        return pl.ds(pl.multiple_of(g * size, size), size)

    @pl.loop(0, groups)
    def _(g):
        load(0, g).wait()
        rows4 = planes(vn, g)
        for r in range(ROWS):
            vpl[at_group(g), COLS * r : COLS * r + COLS] = rows4[r]
        vedge[0, at_group(g), :] = rows4[0].astype(BF16)
        vedge[1, at_group(g), :] = rows4[3].astype(BF16)

    zero_plane = jnp.zeros((GC, COLS), BF16)

    @pl.when(jnp.logical_not(has_up))
    def _():
        @pl.loop(0, groups)
        def _(g):
            vhalo[0, at_group(g), :] = zero_plane
            kp[at_group(g), 0:COLS] = zero_plane

    @pl.when(jnp.logical_not(has_down))
    def _():
        @pl.loop(0, groups)
        def _(g):
            vhalo[1, at_group(g), :] = zero_plane
            kp[at_group(g), 5 * COLS : 6 * COLS] = zero_plane

    pl.semaphore_wait(barrier, sum(length - 1 for _, length in lines))
    signal_line(here.at[0], lines[1])

    def value_halo(way, g):
        return pltpu.make_async_remote_copy(
            src_ref=vedge.at[way, at_group(g), :],
            dst_ref=vhalo.at[1 - way, at_group(g), :],
            send_sem=vsend.at[way],
            recv_sem=vrecv.at[1 - way, g],
            device_id=(frame, row - 1 if way == 0 else row + 1),
            device_id_type=MESH,
        )

    def key_halo(way, g):
        src = COLS if way == 0 else 4 * COLS
        dst = 5 * COLS if way == 0 else 0
        return pltpu.make_async_remote_copy(
            src_ref=kp.at[at_group(g), src : src + COLS],
            dst_ref=kp.at[at_group(g), dst : dst + COLS],
            send_sem=ksend.at[way],
            recv_sem=krecv.at[1 - way, g],
            device_id=(frame, row - 1 if way == 0 else row + 1),
            device_id_type=MESH,
        )

    def send_halos(halo):
        for way, there in ((0, has_up), (1, has_down)):

            @pl.when(there)
            def _():
                @pl.loop(0, groups)
                def _(g):
                    halo(way, g).start()

    def wait_halo(halo, g):
        for way, there in ((1, has_up), (0, has_down)):

            @pl.when(there)
            def _():
                halo(way, g).wait_recv()

    def wait_sent(sem):
        for way, there in ((0, has_up), (1, has_down)):

            @pl.when(there)
            def _():
                pltpu.make_async_copy(vedge.at[way], vedge.at[way], sem.at[way]).wait()

    send_halos(value_halo)

    @pl.loop(0, groups)
    def _(g):
        load(1, g).wait()
        rows4 = planes(kn, g)
        for r in range(ROWS):
            kp[at_group(g), COLS * (r + 1) : COLS * (r + 2)] = jnp.maximum(
                rows4[r], 0.0
            ).astype(BF16)
        mx[pl.ds(pl.multiple_of(g * GK + GC, 32), GK - GC), :] = jnp.ones(
            (GK - GC, ROWS * COLS), BF16
        )

    taps = jnp.concatenate([w_ref[a].astype(F32) for a in range(3)], axis=0)
    taps = jnp.concatenate([taps, jnp.zeros((7, taps.shape[1]), F32)], axis=0)
    channels = taps.shape[1]
    for at in range(0, channels, 128):
        size = min(128, channels - at)
        wt[at : at + size, :] = jnp.concatenate(
            [taps[:, at : at + size].T, jnp.zeros((size, 112), F32)], axis=1
        )

    tap_of = lax.shift_right_logical(lanes((128, 9 * COLS)), 7)
    hot[...] = jnp.where(
        tap_of == lax.broadcasted_iota(jnp.int32, (128, 9 * COLS), 0), 1.0, 0.0
    ).astype(BF16)

    @pl.loop(0, groups)
    def _(g):
        wb[at_group(g), :] = jnp.dot(
            wt[at_group(g), :].astype(BF16), hot[...], preferred_element_type=F32
        ).astype(BF16)

    weights_copy = pltpu.make_async_copy(wb, weights_out, out_sem.at[0])
    weights_copy.start()

    for i in range(1, 4):
        pl.semaphore_wait(here.at[i - 1], lines[i][1] - 1)
        if i < 3:
            signal_line(here.at[i], lines[i + 1])

    owns_two = (row == lax.rem(frame, rows)) & (frame < extra)
    second_unit = n_dev + frame

    def scatter(part, got, at, g):
        second = g * UNITS >= n_dev
        slot = jnp.where(second, 1, 0)
        start = jnp.where(second, (g * UNITS - n_dev) * rows, g * UNITS)
        there = slot * n_dev + me

        def send(i):
            u = g * UNITS + i
            d = start + jnp.where(second, i * rows + i % rows, i)
            return d, pltpu.make_async_remote_copy(
                src_ref=part.at[u],
                dst_ref=got.at[there],
                send_sem=s_sem.at[at],
                recv_sem=r_sem.at[at, slot],
                device_id=d,
                device_id_type=FLAT,
            )

        last = (n_dev // UNITS) - 1
        mine = jnp.where(g > last, frame // UNITS + last + 1, me // UNITS) == g
        mine = mine & ((g <= last) | owns_two)

        @pl.when(mine)
        def _():
            @pl.loop(0, UNITS)
            def _(i):
                d, copy = send(i)

                @pl.when(d != me)
                def _():
                    copy.start()

        @pl.when(jnp.logical_not(mine))
        def _():
            for i in range(UNITS):
                send(i)[1].start()

    def wait_bytes(ref, count, sem):
        pltpu.make_async_copy(ref.at[pl.ds(0, count)], ref.at[pl.ds(0, count)], sem).wait()

    def gather(part, got, every, at):
        def one(slot, u):
            wait_bytes(got, n_dev - 1, r_sem.at[at, slot])
            got[slot * n_dev + me] = part[u]
            every[u] = jnp.sum(got[slot * n_dev : (slot + 1) * n_dev], axis=0)

            def send(d):
                pltpu.make_async_remote_copy(
                    src_ref=every.at[u],
                    dst_ref=every.at[u],
                    send_sem=g_sem.at[at],
                    recv_sem=a_sem.at[at, slot],
                    device_id=d,
                    device_id_type=FLAT,
                ).start()

            others(send)

        one(0, me)

        @pl.when(owns_two)
        def _():
            one(1, second_unit)

    def wait_gathered(every, at):
        wait_bytes(every, n_dev - 1, a_sem.at[at, 0])

        @pl.when(owns_two)
        def _():
            wait_bytes(every, extra - 1, a_sem.at[at, 1])

        @pl.when(jnp.logical_not(owns_two))
        def _():
            wait_bytes(every, extra, a_sem.at[at, 1])

    def wait_sends(at):
        @pl.when(owns_two)
        def _():
            wait_bytes(part1, n_units - 2, s_sem.at[at])
            wait_bytes(got1, 2 * (n_dev - 1), g_sem.at[at])

        @pl.when(jnp.logical_not(owns_two))
        def _():
            wait_bytes(part1, n_units - 1, s_sem.at[at])
            wait_bytes(got1, n_dev - 1, g_sem.at[at])

    @pl.loop(0, groups)
    def _(g):
        wait_halo(value_halo, g)

        @pl.loop(0, GC // 16, unroll=UNROLL)
        def _(i):
            c = pl.ds(pl.multiple_of(g * GC + i * 16, 16), 16)
            six = [vhalo[0, c, :].astype(F32)]
            six += [vpl[c, COLS * r : COLS * (r + 1)] for r in range(ROWS)]
            six += [vhalo[1, c, :].astype(F32)]
            outs = conv16(six, wb[c, :], False)
            o = pl.ds(pl.multiple_of(g * GK + i * 16, 16), 16)
            for r in range(ROWS):
                mf[c, COLS * r : COLS * (r + 1)] = outs[r]
                mx[o, COLS * r : COLS * (r + 1)] = outs[r].astype(BF16)

        full = lax.dot_general(
            kp[at_group(g), COLS : 5 * COLS],
            mx[at_group(g, GK), :],
            (((1,), (1,)), ((), ())),
            preferred_element_type=F32,
        )
        put_units(part1, g * UNITS, pack(full))
        scatter(part1, got1, 0, g)

    send_halos(key_halo)
    @pl.loop(0, groups)
    def _(g):
        load(2, g).wait()
        rows4 = planes(qn, g)
        for r in range(ROWS):
            qp[at_group(g), COLS * r : COLS * (r + 1)] = jnp.maximum(rows4[r], 0.0).astype(BF16)

    @pl.loop(0, groups)
    def _(g):
        load(3, g).wait()
        rows4 = planes(cn, g)
        top = pl.ds(pl.multiple_of(g * GK, GK), GC)
        for r in range(ROWS):
            cp[top, COLS * r : COLS * (r + 1)] = rows4[r].astype(BF16)
        cp[pl.ds(pl.multiple_of(g * GK + GC, 32), GK - GC), :] = jnp.zeros(
            (GK - GC, ROWS * COLS), BF16
        )

    gather(part1, got1, all1, 0)
    wait_gathered(all1, 0)

    @pl.loop(0, groups)
    def _(g):
        packed = take_units(all1, g * UNITS)
        lane = lanes((HD, GK))
        head = lax.shift_right_logical(lane, 5)
        columns = [packed[:, GC + h : GC + h + 1] for h in range(HPG)]
        sums_wide = jnp.zeros((HD, GK), F32)
        for h in range(HPG):
            sums_wide = jnp.where(head == h, columns[h], sums_wide)
        total = jnp.sum(packed, axis=0, keepdims=True)
        weight = jnp.sum(sums_wide, axis=0, keepdims=True)
        mean = total / (weight + EPS * all_tokens)
        mean = jnp.where(lanes((1, GK)) < GC, mean, 0.0)
        means[g] = jnp.broadcast_to(mean, (8, GK))
        centred = spread(packed - sums_wide * mean, False)
        mean_rows = jnp.where(
            lax.shift_right_logical(lanes((16, GK)), 5)
            == lax.broadcasted_iota(jnp.int32, (16, GK), 0),
            mean,
            0.0,
        )
        left = jnp.concatenate([centred, mean_rows], axis=0).astype(BF16)
        cot = cp[at_group(g, GK), :]
        prod = jnp.dot(left, cot, preferred_element_type=F32)
        vpl[at_group(g), :] = prod[:GC]
        stacked = jnp.concatenate([jnp.broadcast_to(c, (HD, 128)) for c in columns], axis=0)
        sums[at_group(g), :] = stacked
        by_head = jnp.where(
            lanes((GC, 128))
            == lax.shift_right_logical(lax.broadcasted_iota(jnp.int32, (GC, 128), 0), 5),
            stacked,
            0.0,
        )
        sums_rows = by_head.T[:16]
        high = sums_rows.astype(BF16)
        low = (sums_rows - high.astype(F32)).astype(BF16)
        qa = qp[at_group(g), :]
        both = jnp.dot(
            jnp.concatenate([high, low], axis=0), qa, preferred_element_type=F32
        )
        inv = 1.0 / (both[:8] + both[16:24] + EPS * all_tokens)
        invs[g] = inv
        down_rows = []
        scaled = []
        for h in range(HPG):
            rows_h = slice(HD * h, HD * h + HD)
            qh = qa[rows_h].astype(F32)
            dot_h = jnp.sum(qh * prod[rows_h], axis=0, keepdims=True)
            inv_h = inv[h : h + 1]
            down_rows.append(
                -(dot_h - EPS * all_tokens * prod[GC + h : GC + h + 1]) * inv_h
            )
            scaled.append((qh * inv_h).astype(BF16))
        down = jnp.concatenate(down_rows + [jnp.zeros((1, ROWS * COLS), F32)], axis=0)
        downs[g] = down * inv
        tail = jnp.concatenate([down, jnp.zeros((GK - GC - 8, ROWS * COLS), F32)], axis=0)
        cp[pl.ds(pl.multiple_of(g * GK + GC, 32), GK - GC), :] = tail.astype(BF16)
        full = lax.dot_general(
            jnp.concatenate(scaled, axis=0),
            cp[at_group(g, GK), :],
            (((1,), (1,)), ((), ())),
            preferred_element_type=F32,
        )
        put_units(part2, g * UNITS, pack(full))
        scatter(part2, got2, 1, g)

    @pl.loop(0, groups)
    def _(g):
        for h in range(HPG):
            c = pl.ds(pl.multiple_of(g * GC + h * HD, HD), HD)
            for r in range(ROWS):
                at = slice(COLS * r, COLS * (r + 1))
                grad = vpl[c, at] * invs[g, h : h + 1, at] + sums[c, :] * downs[g, h : h + 1, at]
                wide[pl.ds(h * HD * ROWS + r, HD, stride=ROWS), :] = jnp.where(
                    qp[c, at].astype(F32) > 0, grad, 0.0
                )
        nat = pl.ds(pl.multiple_of(g * GC * ROWS, GC * ROWS), GC * ROWS)
        qout[nat, :] = wide[...].astype(BF16)

    query_copy = pltpu.make_async_copy(qout, query_out, out_sem.at[1])
    query_copy.start()

    @pl.loop(0, groups)
    def _(g):
        column = means[g].T[:GC, 0:1]
        o = pl.ds(pl.multiple_of(g * GK, GK), GC)
        mx[o, :] = (mf[at_group(g), :] - column).astype(BF16)
        wait_halo(key_halo, g)

    mixed_copy = pltpu.make_async_copy(mx, mixed_out, out_sem.at[2])
    mixed_copy.start()
    key_copy = pltpu.make_async_copy(kp, key_out, out_sem.at[3])
    key_copy.start()

    gather(part2, got2, all2, 1)
    wait_gathered(all2, 1)
    state_copy = pltpu.make_async_copy(all2, state_out, out_sem.at[4])
    state_copy.start()
    wait_sent(vsend)
    wait_sent(ksend)
    wait_sends(0)
    wait_sends(1)
    weights_copy.wait()
    query_copy.wait()
    mixed_copy.wait()
    key_copy.wait()
    state_copy.wait()


def second_kernel(state, mixed, keys, weights, query_in, gq, gk, gv, wide, mapped):
    gq[...] = query_in[...]
    packed = take_units(state, 0)
    left = spread(packed, True).astype(BF16)
    grad_key = jnp.dot(left, mixed[...], preferred_element_type=F32)
    for r in range(ROWS):
        part = grad_key[:, COLS * r : COLS * (r + 1)]
        wide[pl.ds(r, GC, stride=ROWS), :] = jnp.where(
            keys[:, COLS * (r + 1) : COLS * (r + 2)].astype(F32) > 0, part, 0.0
        )
    gk[...] = wide[...].astype(BF16)
    turned = jnp.concatenate([packed] * 4, axis=0).T[:GC]
    turned = jnp.concatenate([turned, turned], axis=1)
    head = lax.shift_right_logical(lax.broadcasted_iota(jnp.int32, (GC, GK), 0), 5)
    turned = jnp.where(head == lax.shift_right_logical(lanes((GC, GK)), 5), turned, 0.0)
    mapped[...] = jnp.dot(
        turned[:, :GC].astype(BF16), keys[...], preferred_element_type=F32
    )

    @pl.loop(0, GC // 16, unroll=UNROLL)
    def _(i):
        c = pl.ds(pl.multiple_of(i * 16, 16), 16)
        six = [mapped[c, COLS * r : COLS * (r + 1)] for r in range(ROWS + 2)]
        outs = conv16(six, weights[c, :], True)
        for r in range(ROWS):
            wide[pl.ds(i * 16 * ROWS + r, 16, stride=ROWS), :] = outs[r]

    gv[...] = wide[...].astype(BF16)


def shards(frames, rows, query_pre, key_pre, values, cotangent, kernel):
    channels = values.shape[0]
    groups = channels // GC
    flat = (channels * ROWS, COLS)
    tokens = ROWS * COLS
    all_tokens = tokens * frames * rows
    n_units = groups * UNITS
    n_dev = frames * rows
    hbm = pl.BlockSpec(memory_space=pl.ANY)
    unit = (4, 128)
    state, mixed, keys, query, weights = pl.pallas_call(
        functools.partial(first_kernel, frames, rows, all_tokens),
        out_shape=(
            jax.ShapeDtypeStruct((n_units, *unit), F32),
            jax.ShapeDtypeStruct((groups * GK, tokens), BF16),
            jax.ShapeDtypeStruct((channels, 6 * COLS), BF16),
            jax.ShapeDtypeStruct(flat, BF16),
            jax.ShapeDtypeStruct((channels, 9 * COLS), BF16),
        ),
        in_specs=[hbm] * 4 + [pl.BlockSpec(memory_space=pltpu.VMEM)],
        out_specs=(hbm,) * 5,
        scratch_shapes=[
            pltpu.VMEM(flat, BF16),
            pltpu.VMEM(flat, BF16),
            pltpu.VMEM(flat, BF16),
            pltpu.VMEM(flat, BF16),
            pltpu.VMEM((GC * ROWS, COLS), F32),
            pltpu.VMEM((channels, tokens), F32),
            pltpu.VMEM((2, channels, COLS), BF16),
            pltpu.VMEM((2, channels, COLS), BF16),
            pltpu.VMEM((channels, 6 * COLS), BF16),
            pltpu.VMEM((channels, tokens), BF16),
            pltpu.VMEM((groups * GK, tokens), BF16),
            pltpu.VMEM((channels, tokens), F32),
            pltpu.VMEM((groups * GK, tokens), BF16),
            pltpu.VMEM((channels, 128), F32),
            pltpu.VMEM((channels, 9 * COLS), BF16),
            pltpu.VMEM((128, 9 * COLS), BF16),
            pltpu.VMEM((channels, 128), F32),
            pltpu.VMEM((groups, 8, tokens), F32),
            pltpu.VMEM((groups, 8, tokens), F32),
            pltpu.VMEM((n_units, *unit), F32),
            pltpu.VMEM((n_units, *unit), F32),
            pltpu.VMEM((2 * n_dev, *unit), F32),
            pltpu.VMEM((2 * n_dev, *unit), F32),
            pltpu.VMEM((n_units, *unit), F32),
            pltpu.VMEM((n_units, *unit), F32),
            pltpu.VMEM((groups, 8, GK), F32),
            pltpu.VMEM(flat, BF16),
            pltpu.SemaphoreType.REGULAR((3,)),
            pltpu.SemaphoreType.DMA((4, groups)),
            pltpu.SemaphoreType.DMA((5,)),
            pltpu.SemaphoreType.DMA((2,)),
            pltpu.SemaphoreType.DMA((2, groups)),
            pltpu.SemaphoreType.DMA((2,)),
            pltpu.SemaphoreType.DMA((2, groups)),
            pltpu.SemaphoreType.DMA((2,)),
            pltpu.SemaphoreType.DMA((2, 2)),
            pltpu.SemaphoreType.DMA((2,)),
            pltpu.SemaphoreType.DMA((2, 2)),
        ],
        compiler_params=pltpu.CompilerParams(
            collective_id=0, has_side_effects=True, vmem_limit_bytes=56 * 2**20
        ),
    )(
        query_pre.reshape(flat),
        key_pre.reshape(flat),
        values.reshape(flat),
        cotangent.reshape(flat),
        kernel,
    )
    nat = pl.BlockSpec((GC * ROWS, COLS), lambda g: (g, 0))
    gq, gk, gv = pl.pallas_call(
        second_kernel,
        grid=(groups,),
        out_shape=(jax.ShapeDtypeStruct(flat, BF16),) * 3,
        in_specs=[
            pl.BlockSpec((UNITS, *unit), lambda g: (g, 0, 0)),
            pl.BlockSpec((GK, tokens), lambda g: (g, 0)),
            pl.BlockSpec((GC, 6 * COLS), lambda g: (g, 0)),
            pl.BlockSpec((GC, 9 * COLS), lambda g: (g, 0)),
            nat,
        ],
        out_specs=(nat,) * 3,
        scratch_shapes=[
            pltpu.VMEM((GC * ROWS, COLS), F32),
            pltpu.VMEM((GC, 6 * COLS), F32),
        ],
    )(state, mixed, keys, weights, query)
    return tuple(o.reshape(values.shape) for o in (gq, gk, gv))


def solution(mesh):
    frames, rows = mesh.shape["frame"], mesh.shape["row"]
    spec = P(None, "frame", "row", None)
    return jax.shard_map(
        functools.partial(shards, frames, rows),
        mesh=mesh,
        in_specs=(spec, spec, spec, spec, P()),
        out_specs=(spec, spec, spec),
        check_vma=False,
    )
```

```python
import functools

import jax
import jax.numpy as jnp
from jax import lax
from jax.experimental import pallas as pl
from jax.experimental.pallas import tpu as pltpu
from jax.sharding import PartitionSpec as P

HD = 32
HPG = 7
GC = HPG * HD
GK = 256
COLS = 128
ROWS = 4
UNITS = 8
EPS = 0.001
VMEM_FIRST = 44 * 2**20
VMEM_SECOND = 16 * 2**20
MESH = pl.DeviceIdType.MESH
FLAT = pl.DeviceIdType.LOGICAL
F32 = jnp.float32
BF16 = jnp.bfloat16


def lanes(shape):
    return lax.broadcasted_iota(jnp.int32, shape, len(shape) - 1)


def conv8(rows, taps, flipped):
    outs = []
    for r in range(ROWS):
        sums = []
        for b in range(3):
            total = None
            for a in range(3):
                term = taps[(2 - a) * 3 + 2 - b if flipped else a * 3 + b] * rows[r + a]
                total = term if total is None else total + term
            sums.append(total)
        outs.append(sums[1] + pltpu.roll(sums[0], 1, 1) + pltpu.roll(sums[2], COLS - 1, 1))
    return outs


def one_hot(flipped):
    lane = lanes((128, 9 * COLS))
    tap, at = lax.shift_right_logical(lane, 7), lane & (COLS - 1)
    side = tap - 3 * (tap // 3)
    first, last = (0, COLS - 1) if flipped else (COLS - 1, 0)
    keep = tap == lax.broadcasted_iota(jnp.int32, lane.shape, 0)
    keep = keep & jnp.logical_not((side == 0) & (at == first))
    keep = keep & jnp.logical_not((side == 2) & (at == last))
    return jnp.where(keep, 1.0, 0.0).astype(BF16)


def tap_rows(ref, c):
    return [ref[c, COLS * i : COLS * i + COLS] for i in range(9)]


def pack(full):
    lane = lanes((HD, 128))
    block = lax.shift_right_logical(lane, 5)
    first = jnp.zeros((HD, 128), F32)
    second = jnp.zeros((HD, 128), F32)
    for h in range(HPG):
        rows = slice(HD * h, HD * h + HD)
        if h < 4:
            first = jnp.where(block == h, full[rows, :128], first)
        else:
            second = jnp.where(block == h - 4, full[rows, 128:], second)
        second = jnp.where(lane == 96 + h, full[rows, 128:], second)
    return first, second


def put_units(ref, at, packed):
    for t, part in enumerate(packed):
        for k in range(4):
            ref[at + t * 4 + k] = part[8 * k : 8 * k + 8].astype(ref.dtype)


def take_units(ref, at):
    halves = [
        jnp.concatenate([ref[at + t * 4 + k].astype(F32) for k in range(4)], axis=0)
        for t in range(2)
    ]
    return jnp.concatenate(halves, axis=1)


def spread(packed, keep_sums):
    stacked = jnp.concatenate([packed] * HPG, axis=0)
    head = lax.shift_right_logical(lax.broadcasted_iota(jnp.int32, (GC, GK), 0), 5)
    lane = lanes((GC, GK))
    keep = head == lax.shift_right_logical(lane, 5)
    if keep_sums:
        keep = keep | (lane == GC + head)
    return jnp.where(keep, stacked, 0.0)


def first_kernel(
    frames, rows, all_tokens,
    q_hbm, k_hbm, v_hbm, c_hbm, w_hbm,
    all2, mx, kp, qout, wt,
    qn, kn, vn, cn, wide, vpl, vedge, vhalo, qp, cp, mf, taps0, taps1, hot, sums, invs, downs,
    krows, mrows, part1, part2, got1, got2, all1, means,
    w_ref, here, in_sem, w_sem, vsend, vrecv, ksend, krecv, s_sem, r_sem, g_sem, a_sem,
):
    groups = vpl.shape[0] // GC
    n_dev = frames * rows
    frame, row = lax.axis_index("frame"), lax.axis_index("row")
    me = frame * rows + row
    has_up, has_down = row > 0, row < rows - 1
    n_units = groups * UNITS

    half = n_dev // 2
    even = lax.rem(me, 2) == 0
    owns = even | (lax.rem(me, 8) == 1)
    my_unit = jnp.where(even, me // 2, half + me // 8)
    next_unit = jnp.where(my_unit == n_units - 1, 0, my_unit + 1)
    next_owner = jnp.where(next_unit < half, 2 * next_unit, 8 * (next_unit - half) + 1)

    x, y = frame // 8, lax.rem(frame // 2, 4)
    z, core = lax.rem(frame, 2) + 2 * (row // 2), lax.rem(row, 2)
    xs = [lax.rem(x + i, 4) * 32 for i in range(4)]
    ys = [lax.rem(y + i, 4) * 8 for i in range(4)]
    zs = [lax.rem(z + i, 4) for i in range(4)]
    zs = [lax.rem(a, 2) * 4 + a // 2 * 2 for a in zs]
    zcs = [[a + c for a in zs] for c in (core, 1 - core)]
    steps = [
        (a, b, c, d) for a in range(4) for b in range(4) for c in range(4) for d in range(2)
    ][1:]
    steps.sort(key=lambda step: -sum(min(i, 4 - i) for i in step[:3]))

    def others(act):
        for a, b, c, d in steps:
            act(xs[a] + ys[b] + zcs[d][c])

    sources = ((v_hbm, vn), (k_hbm, kn), (q_hbm, qn), (c_hbm, cn))

    def load(i, g):
        src, dst = sources[i]
        at = pl.ds(pl.multiple_of(g * GC * ROWS, GC * ROWS), GC * ROWS)
        return pltpu.make_async_copy(src.at[at], dst.at[at], in_sem.at[i, g])

    def start_loads(i):
        @pl.loop(0, groups)
        def _(g):
            load(i, g).start()

    start_loads(0)
    barrier = pltpu.get_barrier_semaphore()

    lines = ((1, rows), (rows, 2), (2 * rows, 4), (8 * rows, 4))

    def signal_line(sem, line):
        stride, length = line
        at = lax.rem(me // stride, length)
        for i in range(1, length):
            to = me + (lax.rem(at + i, length) - at) * stride
            pl.semaphore_signal(sem, inc=1, device_id=to, device_id_type=FLAT)

    for line in lines:
        signal_line(barrier, line)
    w_copy = pltpu.make_async_copy(w_hbm, w_ref, w_sem)
    w_copy.start()
    for i in range(1, 4):
        start_loads(i)

    def planes(nat, g):
        at = pl.multiple_of(g * GC * ROWS, GC * ROWS)
        wide[...] = nat[pl.ds(at, GC * ROWS), :].astype(F32)
        return [wide[pl.ds(r, GC, stride=ROWS), :] for r in range(ROWS)]

    def at_group(g, size=GC):
        return pl.ds(pl.multiple_of(g * size, size), size)

    @pl.loop(0, groups)
    def _(g):
        load(0, g).wait()
        rows4 = planes(vn, g)
        for r in range(ROWS):
            vpl[at_group(g), COLS * r : COLS * r + COLS] = rows4[r]
        vedge[0, at_group(g), :] = rows4[0].astype(BF16)
        vedge[1, at_group(g), :] = rows4[3].astype(BF16)

    pl.semaphore_wait(barrier, sum(length - 1 for _, length in lines))
    signal_line(here.at[0], lines[1])

    def value_halo(way, g):
        return pltpu.make_async_remote_copy(
            src_ref=vedge.at[way, at_group(g), :],
            dst_ref=vhalo.at[1 - way, at_group(g), :],
            send_sem=vsend.at[way],
            recv_sem=vrecv.at[1 - way, g],
            device_id=(frame, row - 1 if way == 0 else row + 1),
            device_id_type=MESH,
        )

    def key_halo(way, g):
        src = COLS if way == 0 else 4 * COLS
        dst = 5 * COLS if way == 0 else 0
        return pltpu.make_async_remote_copy(
            src_ref=kp.at[at_group(g), src : src + COLS],
            dst_ref=kp.at[at_group(g), dst : dst + COLS],
            send_sem=ksend.at[way],
            recv_sem=krecv.at[1 - way, g],
            device_id=(frame, row - 1 if way == 0 else row + 1),
            device_id_type=MESH,
        )

    def send_halos(halo):
        for way, there in ((0, has_up), (1, has_down)):

            @pl.when(there)
            def _():
                @pl.loop(0, groups)
                def _(g):
                    halo(way, g).start()

    def wait_halo(halo, g):
        for way, there in ((1, has_up), (0, has_down)):

            @pl.when(there)
            def _():
                halo(way, g).wait_recv()

    def wait_sent(sem):
        for way, there in ((0, has_up), (1, has_down)):

            @pl.when(there)
            def _():
                pltpu.make_async_copy(vedge.at[way], vedge.at[way], sem.at[way]).wait()

    send_halos(value_halo)

    zero_plane = jnp.zeros((GC, COLS), BF16)

    @pl.when(jnp.logical_not(has_up))
    def _():
        @pl.loop(0, groups)
        def _(g):
            vhalo[0, at_group(g), :] = zero_plane
            kp[at_group(g), 0:COLS] = zero_plane

    @pl.when(jnp.logical_not(has_down))
    def _():
        @pl.loop(0, groups)
        def _(g):
            vhalo[1, at_group(g), :] = zero_plane
            kp[at_group(g), 5 * COLS : 6 * COLS] = zero_plane


    @pl.loop(0, groups)
    def _(g):
        load(1, g).wait()
        rows4 = planes(kn, g)
        for r in range(ROWS):
            kp[at_group(g), COLS * (r + 1) : COLS * (r + 2)] = jnp.maximum(
                rows4[r], 0.0
            ).astype(BF16)
        mx[pl.ds(pl.multiple_of(g * GK + GC, 32), GK - GC), :] = jnp.ones(
            (GK - GC, ROWS * COLS), BF16
        )

    w_copy.wait()
    taps = jnp.concatenate([w_ref[a].astype(F32) for a in range(3)], axis=0)
    taps = jnp.concatenate([taps, jnp.zeros((7, taps.shape[1]), F32)], axis=0)
    channels = taps.shape[1]
    for at in range(0, channels, 128):
        size = min(128, channels - at)
        wt[at : at + size, :] = jnp.concatenate(
            [taps[:, at : at + size].T, jnp.zeros((size, 112), F32)], axis=1
        )

    hot[...] = one_hot(False)

    def make_taps(ref, g):
        ref[...] = jnp.dot(
            wt[at_group(g), :].astype(BF16), hot[...], preferred_element_type=F32
        )

    make_taps(taps0, 0)

    for i in range(1, 4):
        pl.semaphore_wait(here.at[i - 1], lines[i][1] - 1)
        if i < 3:
            signal_line(here.at[i], lines[i + 1])

    def scatter(part, got, at, g):
        second = g * UNITS >= half
        start = jnp.where(second, (g * UNITS - half) * 8 + 1, g * UNITS * 2)
        for i in range(UNITS):
            d = start + jnp.where(second, i * 8, i * 2)
            own = d == me
            pltpu.make_async_remote_copy(
                src_ref=part.at[g * UNITS + i],
                dst_ref=got.at[jnp.where(own, n_dev, me)],
                send_sem=s_sem.at[at],
                recv_sem=r_sem.at[at],
                device_id=jnp.where(own, next_owner, d),
                device_id_type=FLAT,
            ).start()

    def wait_bytes(ref, count, sem):
        pltpu.make_async_copy(ref.at[pl.ds(0, count)], ref.at[pl.ds(0, count)], sem).wait()

    def gather(part, got, every, at):
        @pl.when(owns)
        def _():
            wait_bytes(got, n_dev, r_sem.at[at])
            got[me] = part[my_unit]
            total = jnp.sum(got[:n_dev].astype(F32), axis=0)
            every[my_unit] = total.astype(every.dtype)

            def send(d):
                pltpu.make_async_remote_copy(
                    src_ref=every.at[my_unit],
                    dst_ref=every.at[my_unit],
                    send_sem=g_sem.at[at],
                    recv_sem=a_sem.at[at],
                    device_id=d,
                    device_id_type=FLAT,
                ).start()

            others(send)
            wait_bytes(every, n_units - 1, a_sem.at[at])

        @pl.when(jnp.logical_not(owns))
        def _():
            wait_bytes(every, n_units, a_sem.at[at])

    def wait_sends(part, got, at):
        wait_bytes(part, n_units, s_sem.at[at])

        @pl.when(owns)
        def _():
            wait_bytes(got, n_dev - 1, g_sem.at[at])

    def mix(g, taps, next_taps):
        make_taps(next_taps, jnp.minimum(g + 1, groups - 1))
        for i in range(GC // 16):
            c = pl.ds(pl.multiple_of(g * GC + i * 16, 16), 16)
            edge = [vhalo[w, c, :].astype(F32) for w in range(2)]
            both = []
            for k in range(2):
                c8 = pl.ds(pl.multiple_of(g * GC + i * 16 + k * 8, 8), 8)
                six = [edge[0][8 * k : 8 * k + 8]]
                six += [vpl[c8, COLS * r : COLS * (r + 1)] for r in range(ROWS)]
                six += [edge[1][8 * k : 8 * k + 8]]
                outs = conv8(six, tap_rows(taps, slice(i * 16 + k * 8, i * 16 + k * 8 + 8)), False)
                for r in range(ROWS):
                    mf[c8, COLS * r : COLS * (r + 1)] = outs[r]
                both.append(outs)
            o = pl.ds(pl.multiple_of(g * GK + i * 16, 16), 16)
            for r in range(ROWS):
                mx[o, COLS * r : COLS * (r + 1)] = jnp.concatenate(
                    [both[0][r], both[1][r]], axis=0
                ).astype(BF16)
        full = lax.dot_general(
            kp[at_group(g), COLS : 5 * COLS],
            mx[at_group(g, GK), :],
            (((1,), (1,)), ((), ())),
            preferred_element_type=F32,
        )
        put_units(part1, g * UNITS, pack(full))

    @pl.loop(0, groups // 2)
    def _(i):
        wait_halo(value_halo, 2 * i)
        wait_halo(value_halo, 2 * i + 1)
        mix(2 * i, taps0, taps1)
        mix(2 * i + 1, taps1, taps0)
        scatter(part1, got1, 0, 2 * i)
        scatter(part1, got1, 0, 2 * i + 1)

    send_halos(key_halo)
    @pl.loop(0, groups)
    def _(g):
        load(2, g).wait()
        rows4 = planes(qn, g)
        for r in range(ROWS):
            qp[at_group(g), COLS * r : COLS * (r + 1)] = jnp.maximum(rows4[r], 0.0).astype(BF16)

    @pl.loop(0, groups)
    def _(g):
        load(3, g).wait()
        rows4 = planes(cn, g)
        top = pl.ds(pl.multiple_of(g * GK, GK), GC)
        for r in range(ROWS):
            cp[top, COLS * r : COLS * (r + 1)] = rows4[r].astype(BF16)
        cp[pl.ds(pl.multiple_of(g * GK + GC, 32), GK - GC), :] = jnp.zeros(
            (GK - GC, ROWS * COLS), BF16
        )

    gather(part1, got1, all1, 0)

    @pl.loop(0, groups, unroll=2)
    def _(g):
        packed = take_units(all1, g * UNITS)
        lane = lanes((HD, GK))
        head = lax.shift_right_logical(lane, 5)
        columns = [packed[:, GC + h : GC + h + 1] for h in range(HPG)]
        sums_wide = jnp.zeros((HD, GK), F32)
        for h in range(HPG):
            sums_wide = jnp.where(head == h, columns[h], sums_wide)
        total = jnp.sum(packed, axis=0, keepdims=True)
        weight = jnp.sum(sums_wide, axis=0, keepdims=True)
        mean = total / (weight + EPS * all_tokens)
        mean = jnp.where(lanes((1, GK)) < GC, mean, 0.0)
        means[g] = jnp.broadcast_to(mean, (8, GK))
        centred = spread(packed - sums_wide * mean, False)
        mean_rows = jnp.where(
            lax.shift_right_logical(lanes((16, GK)), 5)
            == lax.broadcasted_iota(jnp.int32, (16, GK), 0),
            mean,
            0.0,
        )
        left = jnp.concatenate([centred, mean_rows], axis=0).astype(BF16)
        cot = cp[at_group(g, GK), :]
        prod = jnp.dot(left, cot, preferred_element_type=F32)
        vpl[at_group(g), :] = prod[:GC]
        mrows[g] = prod[GC : GC + 8]
        stacked = jnp.concatenate([jnp.broadcast_to(c, (HD, 128)) for c in columns], axis=0)
        sums[at_group(g), :] = stacked
        by_head = jnp.where(
            lanes((GC, 128))
            == lax.shift_right_logical(lax.broadcasted_iota(jnp.int32, (GC, 128), 0), 5),
            stacked,
            0.0,
        )
        sums_rows = by_head.T[:16]
        high = sums_rows.astype(BF16)
        low = (sums_rows - high.astype(F32)).astype(BF16)
        krows[g] = jnp.concatenate([high, low], axis=0)

    def grads_of_state(g):
        qa = qp[at_group(g), :]
        both = jnp.dot(krows[g], qa, preferred_element_type=F32)
        inv = 1.0 / (both[:8] + both[16:24] + EPS * all_tokens)
        invs[g] = inv
        down_rows = []
        scaled = []
        for h in range(HPG):
            rows_h = slice(HD * h, HD * h + HD)
            qh = qa[rows_h].astype(F32)
            ph = vpl[pl.ds(pl.multiple_of(g * GC + h * HD, HD), HD), :]
            dot_h = jnp.sum(qh * ph, axis=0, keepdims=True)
            inv_h = inv[h : h + 1]
            down_rows.append(
                -(dot_h - EPS * all_tokens * mrows[g, h : h + 1]) * inv_h
            )
            scaled.append((qh * inv_h).astype(BF16))
        down = jnp.concatenate(down_rows + [jnp.zeros((1, ROWS * COLS), F32)], axis=0)
        downs[g] = down * inv
        tail = jnp.concatenate([down, jnp.zeros((GK - GC - 8, ROWS * COLS), F32)], axis=0)
        cp[pl.ds(pl.multiple_of(g * GK + GC, 32), GK - GC), :] = tail.astype(BF16)
        full = lax.dot_general(
            jnp.concatenate(scaled, axis=0),
            cp[at_group(g, GK), :],
            (((1,), (1,)), ((), ())),
            preferred_element_type=F32,
        )
        put_units(part2, g * UNITS, pack(full))

    @pl.loop(0, groups // 2)
    def _(i):
        grads_of_state(2 * i)
        grads_of_state(2 * i + 1)
        scatter(part2, got2, 1, 2 * i)
        scatter(part2, got2, 1, 2 * i + 1)

    @pl.loop(0, groups)
    def _(g):
        for h in range(HPG):
            c = pl.ds(pl.multiple_of(g * GC + h * HD, HD), HD)
            for r in range(ROWS):
                at = slice(COLS * r, COLS * (r + 1))
                grad = vpl[c, at] * invs[g, h : h + 1, at] + sums[c, :] * downs[g, h : h + 1, at]
                wide[pl.ds(h * HD * ROWS + r, HD, stride=ROWS), :] = jnp.where(
                    qp[c, at].astype(F32) > 0, grad, 0.0
                )
        nat = pl.ds(pl.multiple_of(g * GC * ROWS, GC * ROWS), GC * ROWS)
        qout[nat, :] = wide[...].astype(BF16)

    @pl.loop(0, groups)
    def _(g):
        column = means[g].T[:GC, 0:1]
        o = pl.ds(pl.multiple_of(g * GK, GK), GC)
        mx[o, :] = (mf[at_group(g), :] - column).astype(BF16)
        wait_halo(key_halo, g)

    gather(part2, got2, all2, 1)
    wait_sent(vsend)
    wait_sent(ksend)
    wait_sends(part1, got1, 0)
    wait_sends(part2, got2, 1)


def second_kernel(
    state, mixed, keys, weights, query_in, gq, gk, gv, wide, wide2, mapped, hot, taps
):
    g = pl.program_id(0)
    mine = pl.ds(pl.multiple_of(g * GC, GC), GC)
    nat = pl.ds(pl.multiple_of(g * GC * ROWS, GC * ROWS), GC * ROWS)
    mixed = mixed.at[pl.ds(pl.multiple_of(g * GK, GK), GK)]
    keys = keys.at[mine]

    @pl.when(g == 0)
    def _():
        hot[...] = one_hot(True)

    taps[...] = jnp.dot(weights[mine, :].astype(BF16), hot[...], preferred_element_type=F32)
    gq[...] = query_in[nat, :]
    packed = take_units(state, g * UNITS)
    left = spread(packed, True).astype(BF16)
    grad_key = jnp.dot(left, mixed[...], preferred_element_type=F32)
    for r in range(ROWS):
        part = grad_key[:, COLS * r : COLS * (r + 1)]
        wide[pl.ds(r, GC, stride=ROWS), :] = jnp.where(
            keys[:, COLS * (r + 1) : COLS * (r + 2)].astype(F32) > 0, part, 0.0
        )
    gk[...] = wide[...].astype(BF16)
    turned = jnp.concatenate([packed] * 4, axis=0).T[:GC]
    turned = jnp.concatenate([turned, turned], axis=1)
    head = lax.shift_right_logical(lax.broadcasted_iota(jnp.int32, (GC, GK), 0), 5)
    turned = jnp.where(head == lax.shift_right_logical(lanes((GC, GK)), 5), turned, 0.0)
    mapped[...] = jnp.dot(
        turned[:, :GC].astype(BF16), keys[...], preferred_element_type=F32
    )

    for i in range(GC // 8):
        c = slice(8 * i, 8 * i + 8)
        six = [mapped[c, COLS * r : COLS * (r + 1)] for r in range(ROWS + 2)]
        outs = conv8(six, tap_rows(taps, c), True)
        for r in range(ROWS):
            wide2[pl.ds(i * 8 * ROWS + r, 8, stride=ROWS), :] = outs[r]

    gv[...] = wide2[...].astype(BF16)


def shards(frames, rows, query_pre, key_pre, values, cotangent, kernel):
    channels = values.shape[0]
    groups = channels // GC
    flat = (channels * ROWS, COLS)
    tokens = ROWS * COLS
    all_tokens = tokens * frames * rows
    n_units = groups * UNITS
    n_dev = frames * rows
    hbm = pl.BlockSpec(memory_space=pltpu.HBM)
    vmem = pl.BlockSpec(memory_space=pltpu.VMEM)
    unit = (8, 128)
    state, mixed, keys, query, weights = pl.pallas_call(
        functools.partial(first_kernel, frames, rows, all_tokens),
        out_shape=(
            jax.ShapeDtypeStruct((n_units, *unit), BF16),
            jax.ShapeDtypeStruct((groups * GK, tokens), BF16),
            jax.ShapeDtypeStruct((channels, 6 * COLS), BF16),
            jax.ShapeDtypeStruct(flat, BF16),
            jax.ShapeDtypeStruct((channels, 128), F32),
        ),
        in_specs=[hbm] * 5,
        out_specs=(vmem,) * 5,
        scratch_shapes=[
            pltpu.VMEM(flat, BF16),
            pltpu.VMEM(flat, BF16),
            pltpu.VMEM(flat, BF16),
            pltpu.VMEM(flat, BF16),
            pltpu.VMEM((GC * ROWS, COLS), F32),
            pltpu.VMEM((channels, tokens), F32),
            pltpu.VMEM((2, channels, COLS), BF16),
            pltpu.VMEM((2, channels, COLS), BF16),
            pltpu.VMEM((channels, tokens), BF16),
            pltpu.VMEM((groups * GK, tokens), BF16),
            pltpu.VMEM((channels, tokens), F32),
            pltpu.VMEM((GC, 9 * COLS), F32),
            pltpu.VMEM((GC, 9 * COLS), F32),
            pltpu.VMEM((128, 9 * COLS), BF16),
            pltpu.VMEM((channels, 128), F32),
            pltpu.VMEM((groups, 8, tokens), F32),
            pltpu.VMEM((groups, 8, tokens), F32),
            pltpu.VMEM((groups, 32, GC), BF16),
            pltpu.VMEM((groups, 8, tokens), F32),
            pltpu.VMEM((n_units, *unit), F32),
            pltpu.VMEM((n_units, *unit), BF16),
            pltpu.VMEM((n_dev + 1, *unit), F32),
            pltpu.VMEM((n_dev + 1, *unit), BF16),
            pltpu.VMEM((n_units, *unit), F32),
            pltpu.VMEM((groups, 8, GK), F32),
            pltpu.VMEM((3, 3, channels), BF16),
            pltpu.SemaphoreType.REGULAR((3,)),
            pltpu.SemaphoreType.DMA((4, groups)),
            pltpu.SemaphoreType.DMA,
            pltpu.SemaphoreType.DMA((2,)),
            pltpu.SemaphoreType.DMA((2, groups)),
            pltpu.SemaphoreType.DMA((2,)),
            pltpu.SemaphoreType.DMA((2, groups)),
            pltpu.SemaphoreType.DMA((2,)),
            pltpu.SemaphoreType.DMA((2,)),
            pltpu.SemaphoreType.DMA((2,)),
            pltpu.SemaphoreType.DMA((2,)),
        ],
        compiler_params=pltpu.CompilerParams(
            collective_id=0, has_side_effects=True, vmem_limit_bytes=VMEM_FIRST
        ),
    )(
        pltpu.with_memory_space_constraint(query_pre.reshape(flat), pltpu.HBM),
        pltpu.with_memory_space_constraint(key_pre.reshape(flat), pltpu.HBM),
        pltpu.with_memory_space_constraint(values.reshape(flat), pltpu.HBM),
        pltpu.with_memory_space_constraint(cotangent.reshape(flat), pltpu.HBM),
        pltpu.with_memory_space_constraint(kernel, pltpu.HBM),
    )
    nat = pl.BlockSpec((GC * ROWS, COLS), lambda g: (g, 0))
    gq, gk, gv = pl.pallas_call(
        second_kernel,
        grid=(groups,),
        out_shape=(jax.ShapeDtypeStruct(flat, BF16),) * 3,
        in_specs=[vmem] * 5,
        out_specs=(nat,) * 3,
        scratch_shapes=[
            pltpu.VMEM((GC * ROWS, COLS), F32),
            pltpu.VMEM((GC * ROWS, COLS), F32),
            pltpu.VMEM((GC, 6 * COLS), F32),
            pltpu.VMEM((128, 9 * COLS), BF16),
            pltpu.VMEM((GC, 9 * COLS), F32),
        ],
        compiler_params=pltpu.CompilerParams(vmem_limit_bytes=VMEM_SECOND),
    )(state, mixed, keys, weights, query)
    return tuple(o.reshape(values.shape) for o in (gq, gk, gv))


def solution(mesh):
    frames, rows = mesh.shape["frame"], mesh.shape["row"]
    spec = P(None, "frame", "row", None)
    return jax.shard_map(
        functools.partial(shards, frames, rows),
        mesh=mesh,
        in_specs=(spec, spec, spec, spec, P()),
        out_specs=(spec, spec, spec),
        check_vma=False,
    )
```

```python
import functools

import jax
import jax.numpy as jnp
from jax import lax
from jax.experimental import pallas as pl
from jax.experimental.pallas import tpu as pltpu
from jax.sharding import PartitionSpec as P

HD = 32
HPG = 7
GC = HPG * HD
GK = 256
COLS = 128
ROWS = 4
UNITS = 8
EPS = 0.001
VMEM_FIRST = 44 * 2**20
VMEM_SECOND = 16 * 2**20
MESH = pl.DeviceIdType.MESH
FLAT = pl.DeviceIdType.LOGICAL
F32 = jnp.float32
BF16 = jnp.bfloat16


def lanes(shape):
    return lax.broadcasted_iota(jnp.int32, shape, len(shape) - 1)


def conv8(rows, taps, flipped):
    outs = []
    for r in range(ROWS):
        sums = []
        for b in range(3):
            total = None
            for a in range(3):
                term = taps[(2 - a) * 3 + 2 - b if flipped else a * 3 + b] * rows[r + a]
                total = term if total is None else total + term
            sums.append(total)
        outs.append(sums[1] + pltpu.roll(sums[0], 1, 1) + pltpu.roll(sums[2], COLS - 1, 1))
    return outs


def one_hot(flipped):
    lane = lanes((128, 9 * COLS))
    tap, at = lax.shift_right_logical(lane, 7), lane & (COLS - 1)
    side = tap - 3 * (tap // 3)
    first, last = (0, COLS - 1) if flipped else (COLS - 1, 0)
    keep = tap == lax.broadcasted_iota(jnp.int32, lane.shape, 0)
    keep = keep & jnp.logical_not((side == 0) & (at == first))
    keep = keep & jnp.logical_not((side == 2) & (at == last))
    return jnp.where(keep, 1.0, 0.0).astype(BF16)


def tap_rows(ref, c):
    return [ref[c, COLS * i : COLS * i + COLS] for i in range(9)]


def pack(full):
    lane = lanes((HD, 128))
    block = lax.shift_right_logical(lane, 5)
    first = jnp.zeros((HD, 128), F32)
    second = jnp.zeros((HD, 128), F32)
    for h in range(HPG):
        rows = slice(HD * h, HD * h + HD)
        if h < 4:
            first = jnp.where(block == h, full[rows, :128], first)
        else:
            second = jnp.where(block == h - 4, full[rows, 128:], second)
        second = jnp.where(lane == 96 + h, full[rows, 128:], second)
    return first, second


def put_units(ref, at, packed):
    for t, part in enumerate(packed):
        for k in range(4):
            ref[at + t * 4 + k] = part[8 * k : 8 * k + 8].astype(ref.dtype)


def take_units(ref, at):
    halves = [
        jnp.concatenate([ref[at + t * 4 + k].astype(F32) for k in range(4)], axis=0)
        for t in range(2)
    ]
    return jnp.concatenate(halves, axis=1)


def spread(packed, keep_sums):
    stacked = jnp.concatenate([packed] * HPG, axis=0)
    head = lax.shift_right_logical(lax.broadcasted_iota(jnp.int32, (GC, GK), 0), 5)
    lane = lanes((GC, GK))
    keep = head == lax.shift_right_logical(lane, 5)
    if keep_sums:
        keep = keep | (lane == GC + head)
    return jnp.where(keep, stacked, 0.0)


def first_kernel(
    frames, rows, all_tokens,
    q_hbm, k_hbm, v_hbm, c_hbm, w_hbm,
    all2, mx, kp, qout, wt,
    qn, kn, vn, cn, wide, vpl, vedge, vhalo, qp, cp, mf, taps0, taps1, hot, sums, invs, downs,
    krows, mrows, part1, part2, got1, got2, all1, means,
    w_ref, here, in_sem, w_sem, vsend, vrecv, ksend, krecv, s_sem, r_sem, g_sem, a_sem,
):
    groups = vpl.shape[0] // GC
    n_dev = frames * rows
    frame, row = lax.axis_index("frame"), lax.axis_index("row")
    me = frame * rows + row
    has_up, has_down = row > 0, row < rows - 1
    n_units = groups * UNITS

    half = n_dev // 2
    even = lax.rem(me, 2) == 0
    owns = even | (lax.rem(me, 8) == 1)
    my_unit = jnp.where(even, me // 2, half + me // 8)
    next_unit = jnp.where(my_unit == n_units - 1, 0, my_unit + 1)
    next_owner = jnp.where(next_unit < half, 2 * next_unit, 8 * (next_unit - half) + 1)

    x, y = frame // 8, lax.rem(frame // 2, 4)
    z, core = lax.rem(frame, 2) + 2 * (row // 2), lax.rem(row, 2)
    xs = [lax.rem(x + i, 4) * 32 for i in range(4)]
    ys = [lax.rem(y + i, 4) * 8 for i in range(4)]
    zs = [lax.rem(z + i, 4) for i in range(4)]
    zs = [lax.rem(a, 2) * 4 + a // 2 * 2 for a in zs]
    zcs = [[a + c for a in zs] for c in (core, 1 - core)]
    steps = [
        (a, b, c, d) for a in range(4) for b in range(4) for c in range(4) for d in range(2)
    ][1:]
    steps.sort(key=lambda step: -sum(min(i, 4 - i) for i in step[:3]))

    def others(act):
        for a, b, c, d in steps:
            act(xs[a] + ys[b] + zcs[d][c])

    sources = ((v_hbm, vn), (k_hbm, kn), (q_hbm, qn), (c_hbm, cn))

    def load(i, g):
        src, dst = sources[i]
        at = pl.ds(pl.multiple_of(g * GC * ROWS, GC * ROWS), GC * ROWS)
        return pltpu.make_async_copy(src.at[at], dst.at[at], in_sem.at[i, g])

    def start_loads(i):
        @pl.loop(0, groups)
        def _(g):
            load(i, g).start()

    start_loads(0)
    barrier = pltpu.get_barrier_semaphore()

    lines = ((1, rows), (rows, 2), (2 * rows, 4), (8 * rows, 4))

    def signal_line(sem, line):
        stride, length = line
        at = lax.rem(me // stride, length)
        for i in range(1, length):
            to = me + (lax.rem(at + i, length) - at) * stride
            pl.semaphore_signal(sem, inc=1, device_id=to, device_id_type=FLAT)

    for line in lines:
        signal_line(barrier, line)
    w_copy = pltpu.make_async_copy(w_hbm, w_ref, w_sem)
    w_copy.start()
    for i in range(1, 4):
        start_loads(i)

    def planes(nat, g):
        at = pl.multiple_of(g * GC * ROWS, GC * ROWS)
        wide[...] = nat[pl.ds(at, GC * ROWS), :].astype(F32)
        return [wide[pl.ds(r, GC, stride=ROWS), :] for r in range(ROWS)]

    def at_group(g, size=GC):
        return pl.ds(pl.multiple_of(g * size, size), size)

    @pl.loop(0, groups)
    def _(g):
        load(0, g).wait()
        rows4 = planes(vn, g)
        for r in range(ROWS):
            vpl[at_group(g), COLS * r : COLS * r + COLS] = rows4[r]
        vedge[0, at_group(g), :] = rows4[0].astype(BF16)
        vedge[1, at_group(g), :] = rows4[3].astype(BF16)

    pl.semaphore_wait(barrier, sum(length - 1 for _, length in lines))
    signal_line(here.at[0], lines[1])

    def value_halo(way, g):
        return pltpu.make_async_remote_copy(
            src_ref=vedge.at[way, at_group(g), :],
            dst_ref=vhalo.at[1 - way, at_group(g), :],
            send_sem=vsend.at[way],
            recv_sem=vrecv.at[1 - way, g],
            device_id=(frame, row - 1 if way == 0 else row + 1),
            device_id_type=MESH,
        )

    def key_halo(way, g):
        src = COLS if way == 0 else 4 * COLS
        dst = 5 * COLS if way == 0 else 0
        return pltpu.make_async_remote_copy(
            src_ref=kp.at[at_group(g), src : src + COLS],
            dst_ref=kp.at[at_group(g), dst : dst + COLS],
            send_sem=ksend.at[way],
            recv_sem=krecv.at[1 - way, g],
            device_id=(frame, row - 1 if way == 0 else row + 1),
            device_id_type=MESH,
        )

    def send_halos(halo):
        for way, there in ((0, has_up), (1, has_down)):

            @pl.when(there)
            def _():
                @pl.loop(0, groups)
                def _(g):
                    halo(way, g).start()

    def wait_halo(halo, g):
        for way, there in ((1, has_up), (0, has_down)):

            @pl.when(there)
            def _():
                halo(way, g).wait_recv()

    def wait_sent(sem):
        for way, there in ((0, has_up), (1, has_down)):

            @pl.when(there)
            def _():
                pltpu.make_async_copy(vedge.at[way], vedge.at[way], sem.at[way]).wait()

    send_halos(value_halo)

    zero_plane = jnp.zeros((GC, COLS), BF16)

    @pl.when(jnp.logical_not(has_up))
    def _():
        @pl.loop(0, groups)
        def _(g):
            vhalo[0, at_group(g), :] = zero_plane
            kp[at_group(g), 0:COLS] = zero_plane

    @pl.when(jnp.logical_not(has_down))
    def _():
        @pl.loop(0, groups)
        def _(g):
            vhalo[1, at_group(g), :] = zero_plane
            kp[at_group(g), 5 * COLS : 6 * COLS] = zero_plane


    @pl.loop(0, groups)
    def _(g):
        load(1, g).wait()
        rows4 = planes(kn, g)
        for r in range(ROWS):
            kp[at_group(g), COLS * (r + 1) : COLS * (r + 2)] = jnp.maximum(
                rows4[r], 0.0
            ).astype(BF16)
        mx[pl.ds(pl.multiple_of(g * GK + GC, 32), GK - GC), :] = jnp.ones(
            (GK - GC, ROWS * COLS), BF16
        )

    w_copy.wait()
    taps = jnp.concatenate([w_ref[a].astype(F32) for a in range(3)], axis=0)
    taps = jnp.concatenate([taps, jnp.zeros((7, taps.shape[1]), F32)], axis=0)
    channels = taps.shape[1]
    for at in range(0, channels, 128):
        size = min(128, channels - at)
        wt[at : at + size, :] = jnp.concatenate(
            [taps[:, at : at + size].T, jnp.zeros((size, 112), F32)], axis=1
        )

    hot[...] = one_hot(False)

    def make_taps(ref, g):
        ref[...] = jnp.dot(
            wt[at_group(g), :].astype(BF16), hot[...], preferred_element_type=F32
        )

    make_taps(taps0, 0)

    for i in range(1, 4):
        pl.semaphore_wait(here.at[i - 1], lines[i][1] - 1)
        if i < 3:
            signal_line(here.at[i], lines[i + 1])

    def scatter(part, got, at, g):
        second = g * UNITS >= half
        start = jnp.where(second, (g * UNITS - half) * 8 + 1, g * UNITS * 2)
        for i in range(UNITS):
            d = start + jnp.where(second, i * 8, i * 2)
            own = d == me
            pltpu.make_async_remote_copy(
                src_ref=part.at[g * UNITS + i],
                dst_ref=got.at[jnp.where(own, n_dev, me)],
                send_sem=s_sem.at[at],
                recv_sem=r_sem.at[at],
                device_id=jnp.where(own, next_owner, d),
                device_id_type=FLAT,
            ).start()

    def wait_bytes(ref, count, sem):
        pltpu.make_async_copy(ref.at[pl.ds(0, count)], ref.at[pl.ds(0, count)], sem).wait()

    def gather(part, got, every, at):
        @pl.when(owns)
        def _():
            wait_bytes(got, n_dev, r_sem.at[at])
            got[me] = part[my_unit]
            total = jnp.sum(got[:n_dev].astype(F32), axis=0)
            every[my_unit] = total.astype(every.dtype)

            def send(d):
                pltpu.make_async_remote_copy(
                    src_ref=every.at[my_unit],
                    dst_ref=every.at[my_unit],
                    send_sem=g_sem.at[at],
                    recv_sem=a_sem.at[at],
                    device_id=d,
                    device_id_type=FLAT,
                ).start()

            others(send)
            wait_bytes(every, n_units - 1, a_sem.at[at])

        @pl.when(jnp.logical_not(owns))
        def _():
            wait_bytes(every, n_units, a_sem.at[at])

    def wait_sends(part, got, at):
        wait_bytes(part, n_units, s_sem.at[at])

        @pl.when(owns)
        def _():
            wait_bytes(got, n_dev - 1, g_sem.at[at])

    def mix(g, taps, next_taps):
        make_taps(next_taps, jnp.minimum(g + 1, groups - 1))
        for i in range(GC // 16):
            c = pl.ds(pl.multiple_of(g * GC + i * 16, 16), 16)
            edge = [vhalo[w, c, :].astype(F32) for w in range(2)]
            both = []
            for k in range(2):
                c8 = pl.ds(pl.multiple_of(g * GC + i * 16 + k * 8, 8), 8)
                six = [edge[0][8 * k : 8 * k + 8]]
                six += [vpl[c8, COLS * r : COLS * (r + 1)] for r in range(ROWS)]
                six += [edge[1][8 * k : 8 * k + 8]]
                outs = conv8(six, tap_rows(taps, slice(i * 16 + k * 8, i * 16 + k * 8 + 8)), False)
                for r in range(ROWS):
                    mf[c8, COLS * r : COLS * (r + 1)] = outs[r]
                both.append(outs)
            o = pl.ds(pl.multiple_of(g * GK + i * 16, 16), 16)
            for r in range(ROWS):
                mx[o, COLS * r : COLS * (r + 1)] = jnp.concatenate(
                    [both[0][r], both[1][r]], axis=0
                ).astype(BF16)
        full = lax.dot_general(
            kp[at_group(g), COLS : 5 * COLS],
            mx[at_group(g, GK), :],
            (((1,), (1,)), ((), ())),
            preferred_element_type=F32,
        )
        put_units(part1, g * UNITS, pack(full))

    @pl.loop(0, groups // 2)
    def _(i):
        wait_halo(value_halo, 2 * i)
        wait_halo(value_halo, 2 * i + 1)
        mix(2 * i, taps0, taps1)
        mix(2 * i + 1, taps1, taps0)
        scatter(part1, got1, 0, 2 * i)
        scatter(part1, got1, 0, 2 * i + 1)

    @pl.loop(0, groups)
    def _(g):
        load(2, g).wait()
        rows4 = planes(qn, g)
        for r in range(ROWS):
            qp[at_group(g), COLS * r : COLS * (r + 1)] = jnp.maximum(rows4[r], 0.0).astype(BF16)

    @pl.loop(0, groups)
    def _(g):
        load(3, g).wait()
        rows4 = planes(cn, g)
        top = pl.ds(pl.multiple_of(g * GK, GK), GC)
        for r in range(ROWS):
            cp[top, COLS * r : COLS * (r + 1)] = rows4[r].astype(BF16)
        cp[pl.ds(pl.multiple_of(g * GK + GC, 32), GK - GC), :] = jnp.zeros(
            (GK - GC, ROWS * COLS), BF16
        )

    gather(part1, got1, all1, 0)

    @pl.loop(0, groups, unroll=2)
    def _(g):
        packed = take_units(all1, g * UNITS)
        lane = lanes((HD, GK))
        head = lax.shift_right_logical(lane, 5)
        columns = [packed[:, GC + h : GC + h + 1] for h in range(HPG)]
        sums_wide = jnp.zeros((HD, GK), F32)
        for h in range(HPG):
            sums_wide = jnp.where(head == h, columns[h], sums_wide)
        total = jnp.sum(packed, axis=0, keepdims=True)
        weight = jnp.sum(sums_wide, axis=0, keepdims=True)
        mean = total / (weight + EPS * all_tokens)
        mean = jnp.where(lanes((1, GK)) < GC, mean, 0.0)
        means[g] = jnp.broadcast_to(mean, (8, GK))
        centred = spread(packed - sums_wide * mean, False)
        mean_rows = jnp.where(
            lax.shift_right_logical(lanes((16, GK)), 5)
            == lax.broadcasted_iota(jnp.int32, (16, GK), 0),
            mean,
            0.0,
        )
        left = jnp.concatenate([centred, mean_rows], axis=0).astype(BF16)
        cot = cp[at_group(g, GK), :]
        prod = jnp.dot(left, cot, preferred_element_type=F32)
        vpl[at_group(g), :] = prod[:GC]
        mrows[g] = prod[GC : GC + 8]
        stacked = jnp.concatenate([jnp.broadcast_to(c, (HD, 128)) for c in columns], axis=0)
        sums[at_group(g), :] = stacked
        by_head = jnp.where(
            lanes((GC, 128))
            == lax.shift_right_logical(lax.broadcasted_iota(jnp.int32, (GC, 128), 0), 5),
            stacked,
            0.0,
        )
        sums_rows = by_head.T[:16]
        high = sums_rows.astype(BF16)
        low = (sums_rows - high.astype(F32)).astype(BF16)
        krows[g] = jnp.concatenate([high, low], axis=0)

    def grads_of_state(g):
        qa = qp[at_group(g), :]
        both = jnp.dot(krows[g], qa, preferred_element_type=F32)
        inv = 1.0 / (both[:8] + both[16:24] + EPS * all_tokens)
        invs[g] = inv
        down_rows = []
        scaled = []
        for h in range(HPG):
            rows_h = slice(HD * h, HD * h + HD)
            qh = qa[rows_h].astype(F32)
            ph = vpl[pl.ds(pl.multiple_of(g * GC + h * HD, HD), HD), :]
            dot_h = jnp.sum(qh * ph, axis=0, keepdims=True)
            inv_h = inv[h : h + 1]
            down_rows.append(
                -(dot_h - EPS * all_tokens * mrows[g, h : h + 1]) * inv_h
            )
            scaled.append((qh * inv_h).astype(BF16))
        down = jnp.concatenate(down_rows + [jnp.zeros((1, ROWS * COLS), F32)], axis=0)
        downs[g] = down * inv
        tail = jnp.concatenate([down, jnp.zeros((GK - GC - 8, ROWS * COLS), F32)], axis=0)
        cp[pl.ds(pl.multiple_of(g * GK + GC, 32), GK - GC), :] = tail.astype(BF16)
        full = lax.dot_general(
            jnp.concatenate(scaled, axis=0),
            cp[at_group(g, GK), :],
            (((1,), (1,)), ((), ())),
            preferred_element_type=F32,
        )
        put_units(part2, g * UNITS, pack(full))

    @pl.loop(0, groups // 2)
    def _(i):
        grads_of_state(2 * i)
        grads_of_state(2 * i + 1)
        scatter(part2, got2, 1, 2 * i)
        scatter(part2, got2, 1, 2 * i + 1)

    send_halos(key_halo)

    @pl.loop(0, groups)
    def _(g):
        for h in range(HPG):
            c = pl.ds(pl.multiple_of(g * GC + h * HD, HD), HD)
            for r in range(ROWS):
                at = slice(COLS * r, COLS * (r + 1))
                grad = vpl[c, at] * invs[g, h : h + 1, at] + sums[c, :] * downs[g, h : h + 1, at]
                wide[pl.ds(h * HD * ROWS + r, HD, stride=ROWS), :] = jnp.where(
                    qp[c, at].astype(F32) > 0, grad, 0.0
                )
        nat = pl.ds(pl.multiple_of(g * GC * ROWS, GC * ROWS), GC * ROWS)
        qout[nat, :] = wide[...].astype(BF16)

    @pl.loop(0, groups)
    def _(g):
        column = means[g].T[:GC, 0:1]
        o = pl.ds(pl.multiple_of(g * GK, GK), GC)
        mx[o, :] = (mf[at_group(g), :] - column).astype(BF16)
    gather(part2, got2, all2, 1)

    @pl.loop(0, groups)
    def _(g):
        wait_halo(key_halo, g)

    wait_sent(vsend)
    wait_sent(ksend)
    wait_sends(part1, got1, 0)
    wait_sends(part2, got2, 1)


def second_kernel(
    state, mixed, keys, weights, query_in, gq, gk, gv, wide, wide2, mapped, hot, taps
):
    g = pl.program_id(0)
    mine = pl.ds(pl.multiple_of(g * GC, GC), GC)
    nat = pl.ds(pl.multiple_of(g * GC * ROWS, GC * ROWS), GC * ROWS)
    mixed = mixed.at[pl.ds(pl.multiple_of(g * GK, GK), GK)]
    keys = keys.at[mine]

    @pl.when(g == 0)
    def _():
        hot[...] = one_hot(True)

    taps[...] = jnp.dot(weights[mine, :].astype(BF16), hot[...], preferred_element_type=F32)
    gq[...] = query_in[nat, :]
    packed = take_units(state, g * UNITS)
    left = spread(packed, True).astype(BF16)
    grad_key = jnp.dot(left, mixed[...], preferred_element_type=F32)
    for r in range(ROWS):
        part = grad_key[:, COLS * r : COLS * (r + 1)]
        wide[pl.ds(r, GC, stride=ROWS), :] = jnp.where(
            keys[:, COLS * (r + 1) : COLS * (r + 2)].astype(F32) > 0, part, 0.0
        )
    gk[...] = wide[...].astype(BF16)
    turned = jnp.concatenate([packed] * 4, axis=0).T[:GC]
    turned = jnp.concatenate([turned, turned], axis=1)
    head = lax.shift_right_logical(lax.broadcasted_iota(jnp.int32, (GC, GK), 0), 5)
    turned = jnp.where(head == lax.shift_right_logical(lanes((GC, GK)), 5), turned, 0.0)
    mapped[...] = jnp.dot(
        turned[:, :GC].astype(BF16), keys[...], preferred_element_type=F32
    )

    for i in range(GC // 8):
        c = slice(8 * i, 8 * i + 8)
        six = [mapped[c, COLS * r : COLS * (r + 1)] for r in range(ROWS + 2)]
        outs = conv8(six, tap_rows(taps, c), True)
        for r in range(ROWS):
            wide2[pl.ds(i * 8 * ROWS + r, 8, stride=ROWS), :] = outs[r]

    gv[...] = wide2[...].astype(BF16)


def shards(frames, rows, query_pre, key_pre, values, cotangent, kernel):
    channels = values.shape[0]
    groups = channels // GC
    flat = (channels * ROWS, COLS)
    tokens = ROWS * COLS
    all_tokens = tokens * frames * rows
    n_units = groups * UNITS
    n_dev = frames * rows
    hbm = pl.BlockSpec(memory_space=pltpu.HBM)
    vmem = pl.BlockSpec(memory_space=pltpu.VMEM)
    unit = (8, 128)
    state, mixed, keys, query, weights = pl.pallas_call(
        functools.partial(first_kernel, frames, rows, all_tokens),
        out_shape=(
            jax.ShapeDtypeStruct((n_units, *unit), BF16),
            jax.ShapeDtypeStruct((groups * GK, tokens), BF16),
            jax.ShapeDtypeStruct((channels, 6 * COLS), BF16),
            jax.ShapeDtypeStruct(flat, BF16),
            jax.ShapeDtypeStruct((channels, 128), F32),
        ),
        in_specs=[hbm] * 5,
        out_specs=(vmem,) * 5,
        scratch_shapes=[
            pltpu.VMEM(flat, BF16),
            pltpu.VMEM(flat, BF16),
            pltpu.VMEM(flat, BF16),
            pltpu.VMEM(flat, BF16),
            pltpu.VMEM((GC * ROWS, COLS), F32),
            pltpu.VMEM((channels, tokens), F32),
            pltpu.VMEM((2, channels, COLS), BF16),
            pltpu.VMEM((2, channels, COLS), BF16),
            pltpu.VMEM((channels, tokens), BF16),
            pltpu.VMEM((groups * GK, tokens), BF16),
            pltpu.VMEM((channels, tokens), F32),
            pltpu.VMEM((GC, 9 * COLS), F32),
            pltpu.VMEM((GC, 9 * COLS), F32),
            pltpu.VMEM((128, 9 * COLS), BF16),
            pltpu.VMEM((channels, 128), F32),
            pltpu.VMEM((groups, 8, tokens), F32),
            pltpu.VMEM((groups, 8, tokens), F32),
            pltpu.VMEM((groups, 32, GC), BF16),
            pltpu.VMEM((groups, 8, tokens), F32),
            pltpu.VMEM((n_units, *unit), F32),
            pltpu.VMEM((n_units, *unit), BF16),
            pltpu.VMEM((n_dev + 1, *unit), F32),
            pltpu.VMEM((n_dev + 1, *unit), BF16),
            pltpu.VMEM((n_units, *unit), F32),
            pltpu.VMEM((groups, 8, GK), F32),
            pltpu.VMEM((3, 3, channels), BF16),
            pltpu.SemaphoreType.REGULAR((3,)),
            pltpu.SemaphoreType.DMA((4, groups)),
            pltpu.SemaphoreType.DMA,
            pltpu.SemaphoreType.DMA((2,)),
            pltpu.SemaphoreType.DMA((2, groups)),
            pltpu.SemaphoreType.DMA((2,)),
            pltpu.SemaphoreType.DMA((2, groups)),
            pltpu.SemaphoreType.DMA((2,)),
            pltpu.SemaphoreType.DMA((2,)),
            pltpu.SemaphoreType.DMA((2,)),
            pltpu.SemaphoreType.DMA((2,)),
        ],
        compiler_params=pltpu.CompilerParams(
            collective_id=0, has_side_effects=True, vmem_limit_bytes=VMEM_FIRST
        ),
    )(
        pltpu.with_memory_space_constraint(query_pre.reshape(flat), pltpu.HBM),
        pltpu.with_memory_space_constraint(key_pre.reshape(flat), pltpu.HBM),
        pltpu.with_memory_space_constraint(values.reshape(flat), pltpu.HBM),
        pltpu.with_memory_space_constraint(cotangent.reshape(flat), pltpu.HBM),
        pltpu.with_memory_space_constraint(kernel, pltpu.HBM),
    )
    nat = pl.BlockSpec((GC * ROWS, COLS), lambda g: (g, 0))
    gq, gk, gv = pl.pallas_call(
        second_kernel,
        grid=(groups,),
        out_shape=(jax.ShapeDtypeStruct(flat, BF16),) * 3,
        in_specs=[vmem] * 5,
        out_specs=(nat,) * 3,
        scratch_shapes=[
            pltpu.VMEM((GC * ROWS, COLS), F32),
            pltpu.VMEM((GC * ROWS, COLS), F32),
            pltpu.VMEM((GC, 6 * COLS), F32),
            pltpu.VMEM((128, 9 * COLS), BF16),
            pltpu.VMEM((GC, 9 * COLS), F32),
        ],
        compiler_params=pltpu.CompilerParams(vmem_limit_bytes=VMEM_SECOND),
    )(state, mixed, keys, weights, query)
    return tuple(o.reshape(values.shape) for o in (gq, gk, gv))


def solution(mesh):
    frames, rows = mesh.shape["frame"], mesh.shape["row"]
    spec = P(None, "frame", "row", None)
    return jax.shard_map(
        functools.partial(shards, frames, rows),
        mesh=mesh,
        in_specs=(spec, spec, spec, spec, P()),
        out_specs=(spec, spec, spec),
        check_vma=False,
    )
```

```python
import functools

import jax
import jax.numpy as jnp
from jax import lax
from jax.experimental import pallas as pl
from jax.experimental.pallas import tpu as pltpu
from jax.sharding import PartitionSpec as P

HD = 32
HPG = 7
GC = HPG * HD
GK = 256
COLS = 128
ROWS = 4
UNITS = 8
EPS = 0.001
VMEM_FIRST = 44 * 2**20
VMEM_SECOND = 16 * 2**20
MESH = pl.DeviceIdType.MESH
FLAT = pl.DeviceIdType.LOGICAL
F32 = jnp.float32
BF16 = jnp.bfloat16


def lanes(shape):
    return lax.broadcasted_iota(jnp.int32, shape, len(shape) - 1)


def conv8(rows, taps, flipped):
    outs = []
    for r in range(ROWS):
        sums = []
        for b in range(3):
            total = None
            for a in range(3):
                term = taps[(2 - a) * 3 + 2 - b if flipped else a * 3 + b] * rows[r + a]
                total = term if total is None else total + term
            sums.append(total)
        outs.append(sums[1] + pltpu.roll(sums[0], 1, 1) + pltpu.roll(sums[2], COLS - 1, 1))
    return outs


def one_hot(flipped):
    lane = lanes((128, 9 * COLS))
    tap, at = lax.shift_right_logical(lane, 7), lane & (COLS - 1)
    side = tap - 3 * (tap // 3)
    first, last = (0, COLS - 1) if flipped else (COLS - 1, 0)
    keep = tap == lax.broadcasted_iota(jnp.int32, lane.shape, 0)
    keep = keep & jnp.logical_not((side == 0) & (at == first))
    keep = keep & jnp.logical_not((side == 2) & (at == last))
    return jnp.where(keep, 1.0, 0.0).astype(BF16)


def tap_rows(ref, c):
    return [ref[c, COLS * i : COLS * i + COLS] for i in range(9)]


def pack(full):
    lane = lanes((HD, 128))
    block = lax.shift_right_logical(lane, 5)
    first = jnp.zeros((HD, 128), F32)
    second = jnp.zeros((HD, 128), F32)
    for h in range(HPG):
        rows = slice(HD * h, HD * h + HD)
        if h < 4:
            first = jnp.where(block == h, full[rows, :128], first)
        else:
            second = jnp.where(block == h - 4, full[rows, 128:], second)
        second = jnp.where(lane == 96 + h, full[rows, 128:], second)
    return first, second


def put_units(ref, at, packed):
    for t, part in enumerate(packed):
        for k in range(4):
            ref[at + t * 4 + k] = part[8 * k : 8 * k + 8].astype(ref.dtype)


def take_units(ref, at, apart=4):
    halves = [
        jnp.concatenate([ref[at + t * apart + k].astype(F32) for k in range(4)], axis=0)
        for t in range(2)
    ]
    return jnp.concatenate(halves, axis=1)


def spread(packed, keep_sums):
    stacked = jnp.concatenate([packed] * HPG, axis=0)
    head = lax.shift_right_logical(lax.broadcasted_iota(jnp.int32, (GC, GK), 0), 5)
    lane = lanes((GC, GK))
    keep = head == lax.shift_right_logical(lane, 5)
    if keep_sums:
        keep = keep | (lane == GC + head)
    return jnp.where(keep, stacked, 0.0)


def first_kernel(
    frames, rows, all_tokens,
    q_hbm, k_hbm, v_hbm, c_hbm, w_hbm,
    all2, mx, kp, qout, wt,
    qn, kn, vn, cn, wide, vpl, vedge, vhalo, qp, cp, mf, taps0, taps1, hot, sums, invs, downs,
    krows, mrows, part1, part2, got1, got2, all1, means, pair, both, yard,
    w_ref, here, in_sem, w_sem, vsend, vrecv, ksend, krecv, s_sem, r_sem, g_sem, a_sem,
    pair_send, pair_recv,
):
    groups = vpl.shape[0] // GC
    n_dev = frames * rows
    frame, row = lax.axis_index("frame"), lax.axis_index("row")
    me = frame * rows + row
    has_up, has_down = row > 0, row < rows - 1
    n_units = groups * UNITS

    half = n_dev // 2
    even = lax.rem(me, 2) == 0
    owns = even | (lax.rem(me, 8) == 1)
    my_unit = jnp.where(even, me // 2, half + me // 8)
    next_unit = jnp.where(my_unit == n_units - 1, 0, my_unit + 1)
    next_owner = jnp.where(next_unit < half, 2 * next_unit, 8 * (next_unit - half) + 1)

    x, y = frame // 8, lax.rem(frame // 2, 4)
    z, core = lax.rem(frame, 2) + 2 * (row // 2), lax.rem(row, 2)
    xs = [lax.rem(x + i, 4) * 32 for i in range(4)]
    ys = [lax.rem(y + i, 4) * 8 for i in range(4)]
    zs = [lax.rem(z + i, 4) for i in range(4)]
    zs = [lax.rem(a, 2) * 4 + a // 2 * 2 for a in zs]
    zcs = [[a + c for a in zs] for c in (core, 1 - core)]
    steps = [
        (a, b, c, d) for a in range(4) for b in range(4) for c in range(4) for d in range(2)
    ][1:]
    steps.sort(key=lambda step: -sum(min(i, 4 - i) for i in step[:3]))

    def others(act, same_core=False):
        for a, b, c, d in steps:
            if not (same_core and d):
                act(xs[a] + ys[b] + zcs[d][c])

    chips, n_half = n_dev // 2, n_units // 2
    chip, partner = me // 2, me + 1 - 2 * core
    order = lax.rem(13 * chip, chips)
    again = n_units - chips
    owns_piece = jnp.where(core == 0, order < n_half, (order >= n_half) | (order < again))
    wrapped = jnp.where(order >= n_half, order - n_half, order + chips - n_half)
    my_piece = jnp.where(core == 0, order, wrapped)

    def piece_owner(v):
        return 2 * lax.rem(5 * (v + n_half * core), chips) + core

    next_piece = piece_owner(jnp.where(my_piece == n_half - 1, 0, my_piece + 1))

    sources = ((v_hbm, vn), (k_hbm, kn), (q_hbm, qn), (c_hbm, cn))

    def load(i, g):
        src, dst = sources[i]
        at = pl.ds(pl.multiple_of(g * GC * ROWS, GC * ROWS), GC * ROWS)
        return pltpu.make_async_copy(src.at[at], dst.at[at], in_sem.at[i, g])

    def start_loads(i):
        @pl.loop(0, groups)
        def _(g):
            load(i, g).start()

    start_loads(0)
    barrier = pltpu.get_barrier_semaphore()

    lines = ((1, rows), (rows, 2), (2 * rows, 4), (8 * rows, 4))

    def signal_line(sem, line):
        stride, length = line
        at = lax.rem(me // stride, length)
        for i in range(1, length):
            to = me + (lax.rem(at + i, length) - at) * stride
            pl.semaphore_signal(sem, inc=1, device_id=to, device_id_type=FLAT)

    for line in lines:
        signal_line(barrier, line)
    w_copy = pltpu.make_async_copy(w_hbm, w_ref, w_sem)
    w_copy.start()
    for i in range(1, 4):
        start_loads(i)

    def planes(nat, g):
        at = pl.multiple_of(g * GC * ROWS, GC * ROWS)
        wide[...] = nat[pl.ds(at, GC * ROWS), :].astype(F32)
        return [wide[pl.ds(r, GC, stride=ROWS), :] for r in range(ROWS)]

    def at_group(g, size=GC):
        return pl.ds(pl.multiple_of(g * size, size), size)

    @pl.loop(0, groups)
    def _(g):
        load(0, g).wait()
        rows4 = planes(vn, g)
        for r in range(ROWS):
            vpl[at_group(g), COLS * r : COLS * r + COLS] = rows4[r]
        vedge[0, at_group(g), :] = rows4[0].astype(BF16)
        vedge[1, at_group(g), :] = rows4[3].astype(BF16)

    pl.semaphore_wait(barrier, sum(length - 1 for _, length in lines))
    signal_line(here.at[0], lines[1])

    def value_halo(way, g):
        return pltpu.make_async_remote_copy(
            src_ref=vedge.at[way, at_group(g), :],
            dst_ref=vhalo.at[1 - way, at_group(g), :],
            send_sem=vsend.at[way],
            recv_sem=vrecv.at[1 - way, g],
            device_id=(frame, row - 1 if way == 0 else row + 1),
            device_id_type=MESH,
        )

    def key_halo(way, g):
        src = COLS if way == 0 else 4 * COLS
        dst = 5 * COLS if way == 0 else 0
        return pltpu.make_async_remote_copy(
            src_ref=kp.at[at_group(g), src : src + COLS],
            dst_ref=kp.at[at_group(g), dst : dst + COLS],
            send_sem=ksend.at[way],
            recv_sem=krecv.at[1 - way, g],
            device_id=(frame, row - 1 if way == 0 else row + 1),
            device_id_type=MESH,
        )

    def send_halos(halo):
        for way, there in ((0, has_up), (1, has_down)):

            @pl.when(there)
            def _():
                @pl.loop(0, groups)
                def _(g):
                    halo(way, g).start()

    def wait_halo(halo, g):
        for way, there in ((1, has_up), (0, has_down)):

            @pl.when(there)
            def _():
                halo(way, g).wait_recv()

    def wait_sent(sem):
        for way, there in ((0, has_up), (1, has_down)):

            @pl.when(there)
            def _():
                pltpu.make_async_copy(vedge.at[way], vedge.at[way], sem.at[way]).wait()

    send_halos(value_halo)

    zero_plane = jnp.zeros((GC, COLS), BF16)

    @pl.when(jnp.logical_not(has_up))
    def _():
        @pl.loop(0, groups)
        def _(g):
            vhalo[0, at_group(g), :] = zero_plane
            kp[at_group(g), 0:COLS] = zero_plane

    @pl.when(jnp.logical_not(has_down))
    def _():
        @pl.loop(0, groups)
        def _(g):
            vhalo[1, at_group(g), :] = zero_plane
            kp[at_group(g), 5 * COLS : 6 * COLS] = zero_plane


    @pl.loop(0, groups)
    def _(g):
        load(1, g).wait()
        rows4 = planes(kn, g)
        for r in range(ROWS):
            kp[at_group(g), COLS * (r + 1) : COLS * (r + 2)] = jnp.maximum(
                rows4[r], 0.0
            ).astype(BF16)
        mx[pl.ds(pl.multiple_of(g * GK + GC, 32), GK - GC), :] = jnp.ones(
            (GK - GC, ROWS * COLS), BF16
        )

    w_copy.wait()
    taps = jnp.concatenate([w_ref[a].astype(F32) for a in range(3)], axis=0)
    taps = jnp.concatenate([taps, jnp.zeros((7, taps.shape[1]), F32)], axis=0)
    channels = taps.shape[1]
    for at in range(0, channels, 128):
        size = min(128, channels - at)
        wt[at : at + size, :] = jnp.concatenate(
            [taps[:, at : at + size].T, jnp.zeros((size, 112), F32)], axis=1
        )

    hot[...] = one_hot(False)

    def make_taps(ref, g):
        ref[...] = jnp.dot(
            wt[at_group(g), :].astype(BF16), hot[...], preferred_element_type=F32
        )

    make_taps(taps0, 0)

    for i in range(1, 4):
        pl.semaphore_wait(here.at[i - 1], lines[i][1] - 1)
        if i < 3:
            signal_line(here.at[i], lines[i + 1])

    def scatter(part, got, at, g):
        second = g * UNITS >= half
        start = jnp.where(second, (g * UNITS - half) * 8 + 1, g * UNITS * 2)
        for i in range(UNITS):
            d = start + jnp.where(second, i * 8, i * 2)
            own = d == me
            pltpu.make_async_remote_copy(
                src_ref=part.at[g * UNITS + i],
                dst_ref=got.at[jnp.where(own, n_dev, me)],
                send_sem=s_sem.at[at],
                recv_sem=r_sem.at[at],
                device_id=jnp.where(own, next_owner, d),
                device_id_type=FLAT,
            ).start()

    def pair_copy(g):
        return pltpu.make_async_remote_copy(
            src_ref=part1.at[pl.ds(g * UNITS + 4 * (1 - core), 4)],
            dst_ref=pair.at[pl.ds(g * 4, 4)],
            send_sem=pair_send,
            recv_sem=pair_recv.at[g],
            device_id=partner,
            device_id_type=FLAT,
        )

    def scatter_pieces(g):
        pair_copy(g).wait_recv()
        for k in range(4):
            both[g * 4 + k] = part1[g * UNITS + 4 * core + k] + pair[g * 4 + k]
        for k in range(4):
            d = piece_owner(g * 4 + k)
            own = d == me
            pltpu.make_async_remote_copy(
                src_ref=both.at[g * 4 + k],
                dst_ref=got1.at[jnp.where(own, chips, chip)],
                send_sem=s_sem.at[0],
                recv_sem=r_sem.at[0],
                device_id=jnp.where(own, next_piece, d),
                device_id_type=FLAT,
            ).start()

    def gather_pieces():
        at = core * n_half + my_piece

        @pl.when(owns_piece)
        def _():
            wait_bytes(got1, chips, r_sem.at[0])
            got1[chip] = both[my_piece]
            all1[at] = jnp.sum(got1[:chips], axis=0)

            def send(d):
                pltpu.make_async_remote_copy(
                    src_ref=all1.at[at],
                    dst_ref=all1.at[at],
                    send_sem=g_sem.at[0],
                    recv_sem=a_sem.at[0],
                    device_id=d,
                    device_id_type=FLAT,
                ).start()

            others(send)
            wait_bytes(all1, n_units - 1, a_sem.at[0])

        @pl.when(jnp.logical_not(owns_piece))
        def _():
            wait_bytes(all1, n_units, a_sem.at[0])

    def wait_bytes(ref, count, sem):
        pltpu.make_async_copy(ref.at[pl.ds(0, count)], ref.at[pl.ds(0, count)], sem).wait()

    def gather(part, got, every, at):
        @pl.when(owns)
        def _():
            wait_bytes(got, n_dev, r_sem.at[at])
            got[me] = part[my_unit]
            total = jnp.sum(got[:n_dev].astype(F32), axis=0)
            every[my_unit] = total.astype(every.dtype)

            def send(d):
                pltpu.make_async_remote_copy(
                    src_ref=every.at[my_unit],
                    dst_ref=every.at[my_unit],
                    send_sem=g_sem.at[at],
                    recv_sem=a_sem.at[at],
                    device_id=d,
                    device_id_type=FLAT,
                ).start()

            others(send)
            wait_bytes(every, n_units - 1, a_sem.at[at])

        @pl.when(jnp.logical_not(owns))
        def _():
            wait_bytes(every, n_units, a_sem.at[at])

    def wait_sends():
        wait_bytes(pair, n_half, pair_send)
        wait_bytes(both, n_half, s_sem.at[0])
        wait_bytes(part2, n_units, s_sem.at[1])

        @pl.when(owns_piece)
        def _():
            wait_bytes(yard, n_dev - 1, g_sem.at[0])

        @pl.when(owns)
        def _():
            wait_bytes(got2, n_dev - 1, g_sem.at[1])

    def mix(g, taps, next_taps):
        make_taps(next_taps, jnp.minimum(g + 1, groups - 1))
        for i in range(GC // 16):
            c = pl.ds(pl.multiple_of(g * GC + i * 16, 16), 16)
            edge = [vhalo[w, c, :].astype(F32) for w in range(2)]
            pieces = []
            for k in range(2):
                c8 = pl.ds(pl.multiple_of(g * GC + i * 16 + k * 8, 8), 8)
                six = [edge[0][8 * k : 8 * k + 8]]
                six += [vpl[c8, COLS * r : COLS * (r + 1)] for r in range(ROWS)]
                six += [edge[1][8 * k : 8 * k + 8]]
                outs = conv8(six, tap_rows(taps, slice(i * 16 + k * 8, i * 16 + k * 8 + 8)), False)
                for r in range(ROWS):
                    mf[c8, COLS * r : COLS * (r + 1)] = outs[r]
                pieces.append(outs)
            o = pl.ds(pl.multiple_of(g * GK + i * 16, 16), 16)
            for r in range(ROWS):
                mx[o, COLS * r : COLS * (r + 1)] = jnp.concatenate(
                    [pieces[0][r], pieces[1][r]], axis=0
                ).astype(BF16)
        full = lax.dot_general(
            kp[at_group(g), COLS : 5 * COLS],
            mx[at_group(g, GK), :],
            (((1,), (1,)), ((), ())),
            preferred_element_type=F32,
        )
        put_units(part1, g * UNITS, pack(full))

    @pl.loop(0, groups // 2)
    def _(i):
        wait_halo(value_halo, 2 * i)
        wait_halo(value_halo, 2 * i + 1)
        mix(2 * i, taps0, taps1)
        mix(2 * i + 1, taps1, taps0)
        pair_copy(2 * i).start()
        pair_copy(2 * i + 1).start()

        @pl.when(i > 0)
        def _():
            scatter_pieces(2 * i - 2)
            scatter_pieces(2 * i - 1)

    scatter_pieces(groups - 2)
    scatter_pieces(groups - 1)

    @pl.loop(0, groups)
    def _(g):
        load(2, g).wait()
        rows4 = planes(qn, g)
        for r in range(ROWS):
            qp[at_group(g), COLS * r : COLS * (r + 1)] = jnp.maximum(rows4[r], 0.0).astype(BF16)

    @pl.loop(0, groups)
    def _(g):
        load(3, g).wait()
        rows4 = planes(cn, g)
        top = pl.ds(pl.multiple_of(g * GK, GK), GC)
        for r in range(ROWS):
            cp[top, COLS * r : COLS * (r + 1)] = rows4[r].astype(BF16)
        cp[pl.ds(pl.multiple_of(g * GK + GC, 32), GK - GC), :] = jnp.zeros(
            (GK - GC, ROWS * COLS), BF16
        )

    gather_pieces()

    @pl.loop(0, groups, unroll=2)
    def _(g):
        packed = take_units(all1, g * 4, n_half)
        lane = lanes((HD, GK))
        head = lax.shift_right_logical(lane, 5)
        columns = [packed[:, GC + h : GC + h + 1] for h in range(HPG)]
        sums_wide = jnp.zeros((HD, GK), F32)
        for h in range(HPG):
            sums_wide = jnp.where(head == h, columns[h], sums_wide)
        total = jnp.sum(packed, axis=0, keepdims=True)
        weight = jnp.sum(sums_wide, axis=0, keepdims=True)
        mean = total / (weight + EPS * all_tokens)
        mean = jnp.where(lanes((1, GK)) < GC, mean, 0.0)
        means[g] = jnp.broadcast_to(mean, (8, GK))
        centred = spread(packed - sums_wide * mean, False)
        mean_rows = jnp.where(
            lax.shift_right_logical(lanes((16, GK)), 5)
            == lax.broadcasted_iota(jnp.int32, (16, GK), 0),
            mean,
            0.0,
        )
        left = jnp.concatenate([centred, mean_rows], axis=0).astype(BF16)
        cot = cp[at_group(g, GK), :]
        prod = jnp.dot(left, cot, preferred_element_type=F32)
        vpl[at_group(g), :] = prod[:GC]
        mrows[g] = prod[GC : GC + 8]
        stacked = jnp.concatenate([jnp.broadcast_to(c, (HD, 128)) for c in columns], axis=0)
        sums[at_group(g), :] = stacked
        by_head = jnp.where(
            lanes((GC, 128))
            == lax.shift_right_logical(lax.broadcasted_iota(jnp.int32, (GC, 128), 0), 5),
            stacked,
            0.0,
        )
        sums_rows = by_head.T[:16]
        high = sums_rows.astype(BF16)
        low = (sums_rows - high.astype(F32)).astype(BF16)
        krows[g] = jnp.concatenate([high, low], axis=0)

    def grads_of_state(g):
        qa = qp[at_group(g), :]
        denoms = jnp.dot(krows[g], qa, preferred_element_type=F32)
        inv = 1.0 / (denoms[:8] + denoms[16:24] + EPS * all_tokens)
        invs[g] = inv
        down_rows = []
        scaled = []
        for h in range(HPG):
            rows_h = slice(HD * h, HD * h + HD)
            qh = qa[rows_h].astype(F32)
            ph = vpl[pl.ds(pl.multiple_of(g * GC + h * HD, HD), HD), :]
            dot_h = jnp.sum(qh * ph, axis=0, keepdims=True)
            inv_h = inv[h : h + 1]
            down_rows.append(
                -(dot_h - EPS * all_tokens * mrows[g, h : h + 1]) * inv_h
            )
            scaled.append((qh * inv_h).astype(BF16))
        down = jnp.concatenate(down_rows + [jnp.zeros((1, ROWS * COLS), F32)], axis=0)
        downs[g] = down * inv
        tail = jnp.concatenate([down, jnp.zeros((GK - GC - 8, ROWS * COLS), F32)], axis=0)
        cp[pl.ds(pl.multiple_of(g * GK + GC, 32), GK - GC), :] = tail.astype(BF16)
        full = lax.dot_general(
            jnp.concatenate(scaled, axis=0),
            cp[at_group(g, GK), :],
            (((1,), (1,)), ((), ())),
            preferred_element_type=F32,
        )
        put_units(part2, g * UNITS, pack(full))

    @pl.loop(0, groups // 2)
    def _(i):
        grads_of_state(2 * i)
        grads_of_state(2 * i + 1)
        scatter(part2, got2, 1, 2 * i)
        scatter(part2, got2, 1, 2 * i + 1)

    send_halos(key_halo)

    @pl.loop(0, groups)
    def _(g):
        for h in range(HPG):
            c = pl.ds(pl.multiple_of(g * GC + h * HD, HD), HD)
            for r in range(ROWS):
                at = slice(COLS * r, COLS * (r + 1))
                grad = vpl[c, at] * invs[g, h : h + 1, at] + sums[c, :] * downs[g, h : h + 1, at]
                wide[pl.ds(h * HD * ROWS + r, HD, stride=ROWS), :] = jnp.where(
                    qp[c, at].astype(F32) > 0, grad, 0.0
                )
        nat = pl.ds(pl.multiple_of(g * GC * ROWS, GC * ROWS), GC * ROWS)
        qout[nat, :] = wide[...].astype(BF16)

    @pl.loop(0, groups)
    def _(g):
        column = means[g].T[:GC, 0:1]
        o = pl.ds(pl.multiple_of(g * GK, GK), GC)
        mx[o, :] = (mf[at_group(g), :] - column).astype(BF16)
    gather(part2, got2, all2, 1)

    @pl.loop(0, groups)
    def _(g):
        wait_halo(key_halo, g)

    wait_sent(vsend)
    wait_sent(ksend)
    wait_sends()


def second_kernel(
    state, mixed, keys, weights, query_in, gq, gk, gv, wide, wide2, mapped, hot, taps
):
    g = pl.program_id(0)
    mine = pl.ds(pl.multiple_of(g * GC, GC), GC)
    nat = pl.ds(pl.multiple_of(g * GC * ROWS, GC * ROWS), GC * ROWS)
    mixed = mixed.at[pl.ds(pl.multiple_of(g * GK, GK), GK)]
    keys = keys.at[mine]

    @pl.when(g == 0)
    def _():
        hot[...] = one_hot(True)

    taps[...] = jnp.dot(weights[mine, :].astype(BF16), hot[...], preferred_element_type=F32)
    gq[...] = query_in[nat, :]
    packed = take_units(state, g * UNITS)
    left = spread(packed, True).astype(BF16)
    grad_key = jnp.dot(left, mixed[...], preferred_element_type=F32)
    for r in range(ROWS):
        part = grad_key[:, COLS * r : COLS * (r + 1)]
        wide[pl.ds(r, GC, stride=ROWS), :] = jnp.where(
            keys[:, COLS * (r + 1) : COLS * (r + 2)].astype(F32) > 0, part, 0.0
        )
    gk[...] = wide[...].astype(BF16)
    turned = jnp.concatenate([packed] * 4, axis=0).T[:GC]
    turned = jnp.concatenate([turned, turned], axis=1)
    head = lax.shift_right_logical(lax.broadcasted_iota(jnp.int32, (GC, GK), 0), 5)
    turned = jnp.where(head == lax.shift_right_logical(lanes((GC, GK)), 5), turned, 0.0)
    mapped[...] = jnp.dot(
        turned[:, :GC].astype(BF16), keys[...], preferred_element_type=F32
    )

    for i in range(GC // 8):
        c = slice(8 * i, 8 * i + 8)
        six = [mapped[c, COLS * r : COLS * (r + 1)] for r in range(ROWS + 2)]
        outs = conv8(six, tap_rows(taps, c), True)
        for r in range(ROWS):
            wide2[pl.ds(i * 8 * ROWS + r, 8, stride=ROWS), :] = outs[r]

    gv[...] = wide2[...].astype(BF16)


def shards(frames, rows, query_pre, key_pre, values, cotangent, kernel):
    channels = values.shape[0]
    groups = channels // GC
    flat = (channels * ROWS, COLS)
    tokens = ROWS * COLS
    all_tokens = tokens * frames * rows
    n_units = groups * UNITS
    n_dev = frames * rows
    hbm = pl.BlockSpec(memory_space=pltpu.HBM)
    vmem = pl.BlockSpec(memory_space=pltpu.VMEM)
    unit = (8, 128)
    state, mixed, keys, query, weights = pl.pallas_call(
        functools.partial(first_kernel, frames, rows, all_tokens),
        out_shape=(
            jax.ShapeDtypeStruct((n_units, *unit), BF16),
            jax.ShapeDtypeStruct((groups * GK, tokens), BF16),
            jax.ShapeDtypeStruct((channels, 6 * COLS), BF16),
            jax.ShapeDtypeStruct(flat, BF16),
            jax.ShapeDtypeStruct((channels, 128), F32),
        ),
        in_specs=[hbm] * 5,
        out_specs=(vmem,) * 5,
        scratch_shapes=[
            pltpu.VMEM(flat, BF16),
            pltpu.VMEM(flat, BF16),
            pltpu.VMEM(flat, BF16),
            pltpu.VMEM(flat, BF16),
            pltpu.VMEM((GC * ROWS, COLS), F32),
            pltpu.VMEM((channels, tokens), F32),
            pltpu.VMEM((2, channels, COLS), BF16),
            pltpu.VMEM((2, channels, COLS), BF16),
            pltpu.VMEM((channels, tokens), BF16),
            pltpu.VMEM((groups * GK, tokens), BF16),
            pltpu.VMEM((channels, tokens), F32),
            pltpu.VMEM((GC, 9 * COLS), F32),
            pltpu.VMEM((GC, 9 * COLS), F32),
            pltpu.VMEM((128, 9 * COLS), BF16),
            pltpu.VMEM((channels, 128), F32),
            pltpu.VMEM((groups, 8, tokens), F32),
            pltpu.VMEM((groups, 8, tokens), F32),
            pltpu.VMEM((groups, 32, GC), BF16),
            pltpu.VMEM((groups, 8, tokens), F32),
            pltpu.VMEM((n_units, *unit), F32),
            pltpu.VMEM((n_units, *unit), BF16),
            pltpu.VMEM((n_dev // 2 + 1, *unit), F32),
            pltpu.VMEM((n_dev + 1, *unit), BF16),
            pltpu.VMEM((n_units, *unit), F32),
            pltpu.VMEM((groups, 8, GK), F32),
            pltpu.VMEM((n_units // 2, *unit), F32),
            pltpu.VMEM((n_units // 2, *unit), F32),
            pltpu.VMEM((n_dev, *unit), F32),
            pltpu.VMEM((3, 3, channels), BF16),
            pltpu.SemaphoreType.REGULAR((3,)),
            pltpu.SemaphoreType.DMA((4, groups)),
            pltpu.SemaphoreType.DMA,
            pltpu.SemaphoreType.DMA((2,)),
            pltpu.SemaphoreType.DMA((2, groups)),
            pltpu.SemaphoreType.DMA((2,)),
            pltpu.SemaphoreType.DMA((2, groups)),
            pltpu.SemaphoreType.DMA((2,)),
            pltpu.SemaphoreType.DMA((2,)),
            pltpu.SemaphoreType.DMA((2,)),
            pltpu.SemaphoreType.DMA((2,)),
            pltpu.SemaphoreType.DMA,
            pltpu.SemaphoreType.DMA((groups,)),
        ],
        compiler_params=pltpu.CompilerParams(
            collective_id=0, has_side_effects=True, vmem_limit_bytes=VMEM_FIRST
        ),
    )(
        pltpu.with_memory_space_constraint(query_pre.reshape(flat), pltpu.HBM),
        pltpu.with_memory_space_constraint(key_pre.reshape(flat), pltpu.HBM),
        pltpu.with_memory_space_constraint(values.reshape(flat), pltpu.HBM),
        pltpu.with_memory_space_constraint(cotangent.reshape(flat), pltpu.HBM),
        pltpu.with_memory_space_constraint(kernel, pltpu.HBM),
    )
    nat = pl.BlockSpec((GC * ROWS, COLS), lambda g: (g, 0))
    gq, gk, gv = pl.pallas_call(
        second_kernel,
        grid=(groups,),
        out_shape=(jax.ShapeDtypeStruct(flat, BF16),) * 3,
        in_specs=[vmem] * 5,
        out_specs=(nat,) * 3,
        scratch_shapes=[
            pltpu.VMEM((GC * ROWS, COLS), F32),
            pltpu.VMEM((GC * ROWS, COLS), F32),
            pltpu.VMEM((GC, 6 * COLS), F32),
            pltpu.VMEM((128, 9 * COLS), BF16),
            pltpu.VMEM((GC, 9 * COLS), F32),
        ],
        compiler_params=pltpu.CompilerParams(vmem_limit_bytes=VMEM_SECOND),
    )(state, mixed, keys, weights, query)
    return tuple(o.reshape(values.shape) for o in (gq, gk, gv))


def solution(mesh):
    frames, rows = mesh.shape["frame"], mesh.shape["row"]
    spec = P(None, "frame", "row", None)
    return jax.shard_map(
        functools.partial(shards, frames, rows),
        mesh=mesh,
        in_specs=(spec, spec, spec, spec, P()),
        out_specs=(spec, spec, spec),
        check_vma=False,
    )
```

```python
import functools

import jax
import jax.numpy as jnp
from jax import lax
from jax.experimental import pallas as pl
from jax.experimental.pallas import tpu as pltpu
from jax.sharding import PartitionSpec as P

HD = 32
HPG = 7
GC = HPG * HD
GK = 256
COLS = 128
ROWS = 4
UNITS = 8
EPS = 0.001
VMEM_FIRST = 44 * 2**20
VMEM_SECOND = 16 * 2**20
MESH = pl.DeviceIdType.MESH
FLAT = pl.DeviceIdType.LOGICAL
F32 = jnp.float32
BF16 = jnp.bfloat16


def lanes(shape):
    return lax.broadcasted_iota(jnp.int32, shape, len(shape) - 1)


def conv8(rows, taps, flipped):
    outs = []
    for r in range(ROWS):
        sums = []
        for b in range(3):
            total = None
            for a in range(3):
                term = taps[(2 - a) * 3 + 2 - b if flipped else a * 3 + b] * rows[r + a]
                total = term if total is None else total + term
            sums.append(total)
        outs.append(sums[1] + pltpu.roll(sums[0], 1, 1) + pltpu.roll(sums[2], COLS - 1, 1))
    return outs


def one_hot(flipped):
    lane = lanes((128, 9 * COLS))
    tap, at = lax.shift_right_logical(lane, 7), lane & (COLS - 1)
    side = tap - 3 * (tap // 3)
    first, last = (0, COLS - 1) if flipped else (COLS - 1, 0)
    keep = tap == lax.broadcasted_iota(jnp.int32, lane.shape, 0)
    keep = keep & jnp.logical_not((side == 0) & (at == first))
    keep = keep & jnp.logical_not((side == 2) & (at == last))
    return jnp.where(keep, 1.0, 0.0).astype(BF16)


def tap_rows(ref, c):
    return [ref[c, COLS * i : COLS * i + COLS] for i in range(9)]


def pack(full):
    lane = lanes((HD, 128))
    block = lax.shift_right_logical(lane, 5)
    first = jnp.zeros((HD, 128), F32)
    second = jnp.zeros((HD, 128), F32)
    for h in range(HPG):
        rows = slice(HD * h, HD * h + HD)
        if h < 4:
            first = jnp.where(block == h, full[rows, :128], first)
        else:
            second = jnp.where(block == h - 4, full[rows, 128:], second)
        second = jnp.where(lane == 96 + h, full[rows, 128:], second)
    return first, second


def put_units(ref, at, packed):
    for t, part in enumerate(packed):
        for k in range(4):
            ref[at + t * 4 + k] = part[8 * k : 8 * k + 8].astype(ref.dtype)


def take_units(ref, at, apart=4):
    halves = [
        jnp.concatenate([ref[at + t * apart + k].astype(F32) for k in range(4)], axis=0)
        for t in range(2)
    ]
    return jnp.concatenate(halves, axis=1)


def spread(packed, keep_sums):
    stacked = jnp.concatenate([packed] * HPG, axis=0)
    head = lax.shift_right_logical(lax.broadcasted_iota(jnp.int32, (GC, GK), 0), 5)
    lane = lanes((GC, GK))
    keep = head == lax.shift_right_logical(lane, 5)
    if keep_sums:
        keep = keep | (lane == GC + head)
    return jnp.where(keep, stacked, 0.0)


def first_kernel(
    frames, rows, all_tokens,
    q_hbm, k_hbm, v_hbm, c_hbm, w_hbm,
    all2, mx, kp, qout, wt,
    qn, kn, vn, cn, wide, vpl, vedge, vhalo, qp, cp, mf, taps0, taps1, hot, sums, invs, downs,
    krows, mrows, part1, part2, got1, got2, all1, means, pair, both, yard,
    w_ref, here, in_sem, w_sem, vsend, vrecv, ksend, krecv, s_sem, r_sem, g_sem, a_sem,
    pair_send, pair_recv,
):
    groups = vpl.shape[0] // GC
    n_dev = frames * rows
    frame, row = lax.axis_index("frame"), lax.axis_index("row")
    me = frame * rows + row
    has_up, has_down = row > 0, row < rows - 1
    n_units = groups * UNITS

    half = n_dev // 2
    even = lax.rem(me, 2) == 0
    owns = even | (lax.rem(me, 8) == 1)
    my_unit = jnp.where(even, me // 2, half + me // 8)
    next_unit = jnp.where(my_unit == n_units - 1, 0, my_unit + 1)
    next_owner = jnp.where(next_unit < half, 2 * next_unit, 8 * (next_unit - half) + 1)

    x, y = frame // 8, lax.rem(frame // 2, 4)
    z, core = lax.rem(frame, 2) + 2 * (row // 2), lax.rem(row, 2)
    xs = [lax.rem(x + i, 4) * 32 for i in range(4)]
    ys = [lax.rem(y + i, 4) * 8 for i in range(4)]
    zs = [lax.rem(z + i, 4) for i in range(4)]
    zs = [lax.rem(a, 2) * 4 + a // 2 * 2 for a in zs]
    zcs = [[a + c for a in zs] for c in (core, 1 - core)]
    steps = [
        (a, b, c, d) for a in range(4) for b in range(4) for c in range(4) for d in range(2)
    ][1:]
    steps.sort(key=lambda step: -sum(min(i, 4 - i) for i in step[:3]))

    def others(act, same_core=False):
        for a, b, c, d in steps:
            if not (same_core and d):
                act(xs[a] + ys[b] + zcs[d][c])

    chips, n_half = n_dev // 2, n_units // 2
    chip, partner = me // 2, me + 1 - 2 * core
    order = lax.rem(13 * chip, chips)
    again = n_units - chips
    owns_piece = jnp.where(core == 0, order < n_half, (order >= n_half) | (order < again))
    wrapped = jnp.where(order >= n_half, order - n_half, order + chips - n_half)
    my_piece = jnp.where(core == 0, order, wrapped)

    def piece_owner(v):
        return 2 * lax.rem(5 * (v + n_half * core), chips) + core

    next_piece = piece_owner(jnp.where(my_piece == n_half - 1, 0, my_piece + 1))

    sources = ((v_hbm, vn), (k_hbm, kn), (q_hbm, qn), (c_hbm, cn))

    def load(i, g):
        src, dst = sources[i]
        at = pl.ds(pl.multiple_of(g * GC * ROWS, GC * ROWS), GC * ROWS)
        return pltpu.make_async_copy(src.at[at], dst.at[at], in_sem.at[i, g])

    def start_loads(i):
        @pl.loop(0, groups)
        def _(g):
            load(i, g).start()

    start_loads(0)
    hot[...] = one_hot(False)
    barrier = pltpu.get_barrier_semaphore()

    lines = ((1, rows), (rows, 2), (2 * rows, 4), (8 * rows, 4))

    def signal_line(sem, line):
        stride, length = line
        at = lax.rem(me // stride, length)
        for i in range(1, length):
            to = me + (lax.rem(at + i, length) - at) * stride
            pl.semaphore_signal(sem, inc=1, device_id=to, device_id_type=FLAT)

    for line in lines:
        signal_line(barrier, line)
    w_copy = pltpu.make_async_copy(w_hbm, w_ref, w_sem)
    w_copy.start()
    for i in range(1, 4):
        start_loads(i)

    def planes(nat, g):
        at = pl.multiple_of(g * GC * ROWS, GC * ROWS)
        wide[...] = nat[pl.ds(at, GC * ROWS), :].astype(F32)
        return [wide[pl.ds(r, GC, stride=ROWS), :] for r in range(ROWS)]

    def at_group(g, size=GC):
        return pl.ds(pl.multiple_of(g * size, size), size)

    @pl.loop(0, groups)
    def _(g):
        load(0, g).wait()
        rows4 = planes(vn, g)
        for r in range(ROWS):
            vpl[at_group(g), COLS * r : COLS * r + COLS] = rows4[r]
        vedge[0, at_group(g), :] = rows4[0].astype(BF16)
        vedge[1, at_group(g), :] = rows4[3].astype(BF16)

    pl.semaphore_wait(barrier, sum(length - 1 for _, length in lines))
    signal_line(here.at[0], lines[1])

    def value_halo(way, g):
        return pltpu.make_async_remote_copy(
            src_ref=vedge.at[way, at_group(g), :],
            dst_ref=vhalo.at[1 - way, at_group(g), :],
            send_sem=vsend.at[way],
            recv_sem=vrecv.at[1 - way, g],
            device_id=(frame, row - 1 if way == 0 else row + 1),
            device_id_type=MESH,
        )

    def key_halo(way, g):
        src = COLS if way == 0 else 4 * COLS
        dst = 5 * COLS if way == 0 else 0
        return pltpu.make_async_remote_copy(
            src_ref=kp.at[at_group(g), src : src + COLS],
            dst_ref=kp.at[at_group(g), dst : dst + COLS],
            send_sem=ksend.at[way],
            recv_sem=krecv.at[1 - way, g],
            device_id=(frame, row - 1 if way == 0 else row + 1),
            device_id_type=MESH,
        )

    def send_halos(halo):
        for way, there in ((0, has_up), (1, has_down)):

            @pl.when(there)
            def _():
                @pl.loop(0, groups)
                def _(g):
                    halo(way, g).start()

    def wait_halo(halo, g):
        for way, there in ((1, has_up), (0, has_down)):

            @pl.when(there)
            def _():
                halo(way, g).wait_recv()

    def wait_sent(sem):
        for way, there in ((0, has_up), (1, has_down)):

            @pl.when(there)
            def _():
                pltpu.make_async_copy(vedge.at[way], vedge.at[way], sem.at[way]).wait()

    send_halos(value_halo)

    zero_plane = jnp.zeros((GC, COLS), BF16)

    @pl.when(jnp.logical_not(has_up))
    def _():
        @pl.loop(0, groups)
        def _(g):
            vhalo[0, at_group(g), :] = zero_plane
            kp[at_group(g), 0:COLS] = zero_plane

    @pl.when(jnp.logical_not(has_down))
    def _():
        @pl.loop(0, groups)
        def _(g):
            vhalo[1, at_group(g), :] = zero_plane
            kp[at_group(g), 5 * COLS : 6 * COLS] = zero_plane


    @pl.loop(0, groups)
    def _(g):
        load(1, g).wait()
        rows4 = planes(kn, g)
        for r in range(ROWS):
            kp[at_group(g), COLS * (r + 1) : COLS * (r + 2)] = jnp.maximum(
                rows4[r], 0.0
            ).astype(BF16)
        mx[pl.ds(pl.multiple_of(g * GK + GC, 32), GK - GC), :] = jnp.ones(
            (GK - GC, ROWS * COLS), BF16
        )

    w_copy.wait()
    taps = jnp.concatenate([w_ref[a].astype(F32) for a in range(3)], axis=0)
    taps = jnp.concatenate([taps, jnp.zeros((7, taps.shape[1]), F32)], axis=0)
    channels = taps.shape[1]
    for at in range(0, channels, 128):
        size = min(128, channels - at)
        wt[at : at + size, :] = jnp.concatenate(
            [taps[:, at : at + size].T, jnp.zeros((size, 112), F32)], axis=1
        )

    def make_taps(ref, g):
        ref[...] = jnp.dot(
            wt[at_group(g), :].astype(BF16), hot[...], preferred_element_type=F32
        )

    make_taps(taps0, 0)

    for i in range(1, 4):
        pl.semaphore_wait(here.at[i - 1], lines[i][1] - 1)
        if i < 3:
            signal_line(here.at[i], lines[i + 1])

    def scatter(part, got, at, g):
        second = g * UNITS >= half
        start = jnp.where(second, (g * UNITS - half) * 8 + 1, g * UNITS * 2)
        for i in range(UNITS):
            d = start + jnp.where(second, i * 8, i * 2)
            own = d == me
            pltpu.make_async_remote_copy(
                src_ref=part.at[g * UNITS + i],
                dst_ref=got.at[jnp.where(own, n_dev, me)],
                send_sem=s_sem.at[at],
                recv_sem=r_sem.at[at],
                device_id=jnp.where(own, next_owner, d),
                device_id_type=FLAT,
            ).start()

    def pair_copy(g):
        return pltpu.make_async_remote_copy(
            src_ref=part1.at[pl.ds(g * UNITS + 4 * (1 - core), 4)],
            dst_ref=pair.at[pl.ds(g * 4, 4)],
            send_sem=pair_send,
            recv_sem=pair_recv.at[g],
            device_id=partner,
            device_id_type=FLAT,
        )

    def scatter_pieces(g):
        pair_copy(g).wait_recv()
        for k in range(4):
            both[g * 4 + k] = part1[g * UNITS + 4 * core + k] + pair[g * 4 + k]
        for k in range(4):
            d = piece_owner(g * 4 + k)
            own = d == me
            pltpu.make_async_remote_copy(
                src_ref=both.at[g * 4 + k],
                dst_ref=got1.at[jnp.where(own, chips, chip)],
                send_sem=s_sem.at[0],
                recv_sem=r_sem.at[0],
                device_id=jnp.where(own, next_piece, d),
                device_id_type=FLAT,
            ).start()

    def gather_pieces():
        at = core * n_half + my_piece

        @pl.when(owns_piece)
        def _():
            wait_bytes(got1, chips, r_sem.at[0])
            got1[chip] = both[my_piece]
            all1[at] = jnp.sum(got1[:chips], axis=0)

            def send(d):
                pltpu.make_async_remote_copy(
                    src_ref=all1.at[at],
                    dst_ref=all1.at[at],
                    send_sem=g_sem.at[0],
                    recv_sem=a_sem.at[0],
                    device_id=d,
                    device_id_type=FLAT,
                ).start()

            others(send)
            wait_bytes(all1, n_units - 1, a_sem.at[0])

        @pl.when(jnp.logical_not(owns_piece))
        def _():
            wait_bytes(all1, n_units, a_sem.at[0])

    def wait_bytes(ref, count, sem):
        pltpu.make_async_copy(ref.at[pl.ds(0, count)], ref.at[pl.ds(0, count)], sem).wait()

    def gather(part, got, every, at):
        @pl.when(owns)
        def _():
            wait_bytes(got, n_dev, r_sem.at[at])
            got[me] = part[my_unit]
            total = jnp.sum(got[:n_dev].astype(F32), axis=0)
            every[my_unit] = total.astype(every.dtype)

            def send(d):
                pltpu.make_async_remote_copy(
                    src_ref=every.at[my_unit],
                    dst_ref=every.at[my_unit],
                    send_sem=g_sem.at[at],
                    recv_sem=a_sem.at[at],
                    device_id=d,
                    device_id_type=FLAT,
                ).start()

            others(send)
            wait_bytes(every, n_units - 1, a_sem.at[at])

        @pl.when(jnp.logical_not(owns))
        def _():
            wait_bytes(every, n_units, a_sem.at[at])

    def wait_sends():
        wait_bytes(pair, n_half, pair_send)
        wait_bytes(both, n_half, s_sem.at[0])
        wait_bytes(part2, n_units, s_sem.at[1])

        @pl.when(owns_piece)
        def _():
            wait_bytes(yard, n_dev - 1, g_sem.at[0])

        @pl.when(owns)
        def _():
            wait_bytes(got2, n_dev - 1, g_sem.at[1])

    def mix(g, taps, next_taps):
        make_taps(next_taps, jnp.minimum(g + 1, groups - 1))
        for i in range(GC // 16):
            c = pl.ds(pl.multiple_of(g * GC + i * 16, 16), 16)
            edge = [vhalo[w, c, :].astype(F32) for w in range(2)]
            pieces = []
            for k in range(2):
                c8 = pl.ds(pl.multiple_of(g * GC + i * 16 + k * 8, 8), 8)
                six = [edge[0][8 * k : 8 * k + 8]]
                six += [vpl[c8, COLS * r : COLS * (r + 1)] for r in range(ROWS)]
                six += [edge[1][8 * k : 8 * k + 8]]
                outs = conv8(six, tap_rows(taps, slice(i * 16 + k * 8, i * 16 + k * 8 + 8)), False)
                for r in range(ROWS):
                    mf[c8, COLS * r : COLS * (r + 1)] = outs[r]
                pieces.append(outs)
            o = pl.ds(pl.multiple_of(g * GK + i * 16, 16), 16)
            for r in range(ROWS):
                mx[o, COLS * r : COLS * (r + 1)] = jnp.concatenate(
                    [pieces[0][r], pieces[1][r]], axis=0
                ).astype(BF16)
        full = lax.dot_general(
            kp[at_group(g), COLS : 5 * COLS],
            mx[at_group(g, GK), :],
            (((1,), (1,)), ((), ())),
            preferred_element_type=F32,
        )
        put_units(part1, g * UNITS, pack(full))

    @pl.loop(0, groups // 2)
    def _(i):
        wait_halo(value_halo, 2 * i)
        wait_halo(value_halo, 2 * i + 1)
        mix(2 * i, taps0, taps1)
        mix(2 * i + 1, taps1, taps0)
        pair_copy(2 * i).start()
        pair_copy(2 * i + 1).start()

        @pl.when(i > 0)
        def _():
            scatter_pieces(2 * i - 2)
            scatter_pieces(2 * i - 1)

    scatter_pieces(groups - 2)
    scatter_pieces(groups - 1)

    @pl.loop(0, groups)
    def _(g):
        load(2, g).wait()
        rows4 = planes(qn, g)
        for r in range(ROWS):
            qp[at_group(g), COLS * r : COLS * (r + 1)] = jnp.maximum(rows4[r], 0.0).astype(BF16)

    @pl.loop(0, groups)
    def _(g):
        load(3, g).wait()
        rows4 = planes(cn, g)
        top = pl.ds(pl.multiple_of(g * GK, GK), GC)
        for r in range(ROWS):
            cp[top, COLS * r : COLS * (r + 1)] = rows4[r].astype(BF16)
        cp[pl.ds(pl.multiple_of(g * GK + GC, 32), GK - GC), :] = jnp.zeros(
            (GK - GC, ROWS * COLS), BF16
        )

    gather_pieces()

    @pl.loop(0, groups, unroll=5)
    def _(g):
        packed = take_units(all1, g * 4, n_half)
        lane = lanes((HD, GK))
        head = lax.shift_right_logical(lane, 5)
        columns = [packed[:, GC + h : GC + h + 1] for h in range(HPG)]
        sums_wide = jnp.zeros((HD, GK), F32)
        for h in range(HPG):
            sums_wide = jnp.where(head == h, columns[h], sums_wide)
        total = jnp.sum(packed, axis=0, keepdims=True)
        weight = jnp.sum(sums_wide, axis=0, keepdims=True)
        mean = total / (weight + EPS * all_tokens)
        mean = jnp.where(lanes((1, GK)) < GC, mean, 0.0)
        means[g] = jnp.broadcast_to(mean, (8, GK))
        centred = spread(packed - sums_wide * mean, False)
        mean_rows = jnp.where(
            lax.shift_right_logical(lanes((16, GK)), 5)
            == lax.broadcasted_iota(jnp.int32, (16, GK), 0),
            mean,
            0.0,
        )
        left = jnp.concatenate([centred, mean_rows], axis=0).astype(BF16)
        cot = cp[at_group(g, GK), :]
        prod = jnp.dot(left, cot, preferred_element_type=F32)
        vpl[at_group(g), :] = prod[:GC]
        mrows[g] = prod[GC : GC + 8]
        stacked = jnp.concatenate([jnp.broadcast_to(c, (HD, 128)) for c in columns], axis=0)
        sums[at_group(g), :] = stacked
        by_head = jnp.where(
            lanes((GC, 128))
            == lax.shift_right_logical(lax.broadcasted_iota(jnp.int32, (GC, 128), 0), 5),
            stacked,
            0.0,
        )
        sums_rows = by_head.T[:16]
        high = sums_rows.astype(BF16)
        low = (sums_rows - high.astype(F32)).astype(BF16)
        krows[g] = jnp.concatenate([high, low], axis=0)

    def grads_of_state(g):
        qa = qp[at_group(g), :]
        denoms = jnp.dot(krows[g], qa, preferred_element_type=F32)
        inv = 1.0 / (denoms[:8] + denoms[16:24] + EPS * all_tokens)
        invs[g] = inv
        down_rows = []
        scaled = []
        for h in range(HPG):
            rows_h = slice(HD * h, HD * h + HD)
            qh = qa[rows_h].astype(F32)
            ph = vpl[pl.ds(pl.multiple_of(g * GC + h * HD, HD), HD), :]
            dot_h = jnp.sum(qh * ph, axis=0, keepdims=True)
            inv_h = inv[h : h + 1]
            down_rows.append(
                -(dot_h - EPS * all_tokens * mrows[g, h : h + 1]) * inv_h
            )
            scaled.append((qh * inv_h).astype(BF16))
        down = jnp.concatenate(down_rows + [jnp.zeros((1, ROWS * COLS), F32)], axis=0)
        downs[g] = down * inv
        tail = jnp.concatenate([down, jnp.zeros((GK - GC - 8, ROWS * COLS), F32)], axis=0)
        cp[pl.ds(pl.multiple_of(g * GK + GC, 32), GK - GC), :] = tail.astype(BF16)
        full = lax.dot_general(
            jnp.concatenate(scaled, axis=0),
            cp[at_group(g, GK), :],
            (((1,), (1,)), ((), ())),
            preferred_element_type=F32,
        )
        put_units(part2, g * UNITS, pack(full))

    @pl.loop(0, groups // 5)
    def _(i):
        for k in range(5):
            grads_of_state(5 * i + k)
        for k in range(5):
            scatter(part2, got2, 1, 5 * i + k)

    send_halos(key_halo)

    @pl.loop(0, groups)
    def _(g):
        for h in range(HPG):
            c = pl.ds(pl.multiple_of(g * GC + h * HD, HD), HD)
            for r in range(ROWS):
                at = slice(COLS * r, COLS * (r + 1))
                grad = vpl[c, at] * invs[g, h : h + 1, at] + sums[c, :] * downs[g, h : h + 1, at]
                wide[pl.ds(h * HD * ROWS + r, HD, stride=ROWS), :] = jnp.where(
                    qp[c, at].astype(F32) > 0, grad, 0.0
                )
        nat = pl.ds(pl.multiple_of(g * GC * ROWS, GC * ROWS), GC * ROWS)
        qout[nat, :] = wide[...].astype(BF16)

    @pl.loop(0, groups)
    def _(g):
        column = means[g].T[:GC, 0:1]
        o = pl.ds(pl.multiple_of(g * GK, GK), GC)
        mx[o, :] = (mf[at_group(g), :] - column).astype(BF16)
    gather(part2, got2, all2, 1)

    @pl.loop(0, groups)
    def _(g):
        wait_halo(key_halo, g)

    wait_sent(vsend)
    wait_sent(ksend)
    wait_sends()


def second_kernel(
    state, mixed, keys, weights, query_in, gq, gk, gv, wide, wide2, mapped, hot, taps
):
    g = pl.program_id(0)
    mine = pl.ds(pl.multiple_of(g * GC, GC), GC)
    nat = pl.ds(pl.multiple_of(g * GC * ROWS, GC * ROWS), GC * ROWS)
    mixed = mixed.at[pl.ds(pl.multiple_of(g * GK, GK), GK)]
    keys = keys.at[mine]

    @pl.when(g == 0)
    def _():
        hot[...] = one_hot(True)

    taps[...] = jnp.dot(weights[mine, :].astype(BF16), hot[...], preferred_element_type=F32)
    gq[...] = query_in[nat, :]
    packed = take_units(state, g * UNITS)
    left = spread(packed, True).astype(BF16)
    grad_key = jnp.dot(left, mixed[...], preferred_element_type=F32)
    for r in range(ROWS):
        part = grad_key[:, COLS * r : COLS * (r + 1)]
        wide[pl.ds(r, GC, stride=ROWS), :] = jnp.where(
            keys[:, COLS * (r + 1) : COLS * (r + 2)].astype(F32) > 0, part, 0.0
        )
    gk[...] = wide[...].astype(BF16)
    turned = jnp.concatenate([packed] * 4, axis=0).T[:GC]
    turned = jnp.concatenate([turned, turned], axis=1)
    head = lax.shift_right_logical(lax.broadcasted_iota(jnp.int32, (GC, GK), 0), 5)
    turned = jnp.where(head == lax.shift_right_logical(lanes((GC, GK)), 5), turned, 0.0)
    mapped[...] = jnp.dot(
        turned[:, :GC].astype(BF16), keys[...], preferred_element_type=F32
    )

    for i in range(GC // 8):
        c = slice(8 * i, 8 * i + 8)
        six = [mapped[c, COLS * r : COLS * (r + 1)] for r in range(ROWS + 2)]
        outs = conv8(six, tap_rows(taps, c), True)
        for r in range(ROWS):
            wide2[pl.ds(i * 8 * ROWS + r, 8, stride=ROWS), :] = outs[r]

    gv[...] = wide2[...].astype(BF16)


def shards(frames, rows, query_pre, key_pre, values, cotangent, kernel):
    channels = values.shape[0]
    groups = channels // GC
    flat = (channels * ROWS, COLS)
    tokens = ROWS * COLS
    all_tokens = tokens * frames * rows
    n_units = groups * UNITS
    n_dev = frames * rows
    hbm = pl.BlockSpec(memory_space=pltpu.HBM)
    vmem = pl.BlockSpec(memory_space=pltpu.VMEM)
    unit = (8, 128)
    state, mixed, keys, query, weights = pl.pallas_call(
        functools.partial(first_kernel, frames, rows, all_tokens),
        out_shape=(
            jax.ShapeDtypeStruct((n_units, *unit), BF16),
            jax.ShapeDtypeStruct((groups * GK, tokens), BF16),
            jax.ShapeDtypeStruct((channels, 6 * COLS), BF16),
            jax.ShapeDtypeStruct(flat, BF16),
            jax.ShapeDtypeStruct((channels, 128), F32),
        ),
        in_specs=[hbm] * 5,
        out_specs=(vmem,) * 5,
        scratch_shapes=[
            pltpu.VMEM(flat, BF16),
            pltpu.VMEM(flat, BF16),
            pltpu.VMEM(flat, BF16),
            pltpu.VMEM(flat, BF16),
            pltpu.VMEM((GC * ROWS, COLS), F32),
            pltpu.VMEM((channels, tokens), F32),
            pltpu.VMEM((2, channels, COLS), BF16),
            pltpu.VMEM((2, channels, COLS), BF16),
            pltpu.VMEM((channels, tokens), BF16),
            pltpu.VMEM((groups * GK, tokens), BF16),
            pltpu.VMEM((channels, tokens), F32),
            pltpu.VMEM((GC, 9 * COLS), F32),
            pltpu.VMEM((GC, 9 * COLS), F32),
            pltpu.VMEM((128, 9 * COLS), BF16),
            pltpu.VMEM((channels, 128), F32),
            pltpu.VMEM((groups, 8, tokens), F32),
            pltpu.VMEM((groups, 8, tokens), F32),
            pltpu.VMEM((groups, 32, GC), BF16),
            pltpu.VMEM((groups, 8, tokens), F32),
            pltpu.VMEM((n_units, *unit), F32),
            pltpu.VMEM((n_units, *unit), BF16),
            pltpu.VMEM((n_dev // 2 + 1, *unit), F32),
            pltpu.VMEM((n_dev + 1, *unit), BF16),
            pltpu.VMEM((n_units, *unit), F32),
            pltpu.VMEM((groups, 8, GK), F32),
            pltpu.VMEM((n_units // 2, *unit), F32),
            pltpu.VMEM((n_units // 2, *unit), F32),
            pltpu.VMEM((n_dev, *unit), F32),
            pltpu.VMEM((3, 3, channels), BF16),
            pltpu.SemaphoreType.REGULAR((3,)),
            pltpu.SemaphoreType.DMA((4, groups)),
            pltpu.SemaphoreType.DMA,
            pltpu.SemaphoreType.DMA((2,)),
            pltpu.SemaphoreType.DMA((2, groups)),
            pltpu.SemaphoreType.DMA((2,)),
            pltpu.SemaphoreType.DMA((2, groups)),
            pltpu.SemaphoreType.DMA((2,)),
            pltpu.SemaphoreType.DMA((2,)),
            pltpu.SemaphoreType.DMA((2,)),
            pltpu.SemaphoreType.DMA((2,)),
            pltpu.SemaphoreType.DMA,
            pltpu.SemaphoreType.DMA((groups,)),
        ],
        compiler_params=pltpu.CompilerParams(
            collective_id=0, has_side_effects=True, vmem_limit_bytes=VMEM_FIRST
        ),
    )(
        pltpu.with_memory_space_constraint(query_pre.reshape(flat), pltpu.HBM),
        pltpu.with_memory_space_constraint(key_pre.reshape(flat), pltpu.HBM),
        pltpu.with_memory_space_constraint(values.reshape(flat), pltpu.HBM),
        pltpu.with_memory_space_constraint(cotangent.reshape(flat), pltpu.HBM),
        pltpu.with_memory_space_constraint(kernel, pltpu.HBM),
    )
    nat = pl.BlockSpec((GC * ROWS, COLS), lambda g: (g, 0))
    gq, gk, gv = pl.pallas_call(
        second_kernel,
        grid=(groups,),
        out_shape=(jax.ShapeDtypeStruct(flat, BF16),) * 3,
        in_specs=[vmem] * 5,
        out_specs=(nat,) * 3,
        scratch_shapes=[
            pltpu.VMEM((GC * ROWS, COLS), F32),
            pltpu.VMEM((GC * ROWS, COLS), F32),
            pltpu.VMEM((GC, 6 * COLS), F32),
            pltpu.VMEM((128, 9 * COLS), BF16),
            pltpu.VMEM((GC, 9 * COLS), F32),
        ],
        compiler_params=pltpu.CompilerParams(vmem_limit_bytes=VMEM_SECOND),
    )(state, mixed, keys, weights, query)
    return tuple(o.reshape(values.shape) for o in (gq, gk, gv))


def solution(mesh):
    frames, rows = mesh.shape["frame"], mesh.shape["row"]
    spec = P(None, "frame", "row", None)
    return jax.shard_map(
        functools.partial(shards, frames, rows),
        mesh=mesh,
        in_specs=(spec, spec, spec, spec, P()),
        out_specs=(spec, spec, spec),
        check_vma=False,
    )
```
